32 devices in a mesh: seq: 8 (over z, x), head: 4 (over y, core).
Axes of the slice: x: 2, y: 2, z: 4, core: 2. Of those that a mesh axis runs over, the one named last changes fastest.
Arguments:
- token_ids: int32 [8192], P('seq'), may hold values from 0 to 255
- embedding: bfloat16 [256, 1024], replicated, may hold values from -6 to 6
- fine_norm: float32 [1024], replicated, may hold values from 0.1 to 1.9
- fine_query: bfloat16 [1024, 1024], P(None, 'head'), may hold values from -2 to 2
- fine_key: bfloat16 [1024, 1024], P(None, 'head'), may hold values from -2 to 2
- fine_value: bfloat16 [1024, 1024], P(None, 'head'), may hold values from -0.1875 to 0.1875
- fine_output: bfloat16 [1024, 1024], P('head'), may hold values from -0.1875 to 0.1875
- shorten_weight: bfloat16 [4, 1024, 1024], P(None, 'head'), may hold values from -0.09375 to 0.09375
- coarse_norm: float32 [1024], replicated, may hold values from 0.1 to 1.9
- coarse_query: bfloat16 [1024, 1024], P(None, 'head'), may hold values from -2 to 2
- coarse_key: bfloat16 [1024, 1024], P(None, 'head'), may hold values from -2 to 2
- coarse_value: bfloat16 [1024, 1024], P(None, 'head'), may hold values from -0.1875 to 0.1875
- coarse_output: bfloat16 [1024, 1024], P('head'), may hold values from -0.1875 to 0.1875
- ffn_norm: float32 [1024], replicated, may hold values from 0.1 to 1.9
- ffn_up: bfloat16 [1024, 4096], P(None, 'head'), may hold values from -0.1875 to 0.1875
- ffn_down: bfloat16 [4096, 1024], P('head'), may hold values from -0.09375 to 0.09375
- upsample_weight: bfloat16 [1024, 4, 1024], P(None, None, 'head'), may hold values from -0.1875 to 0.1875
Outputs:
- block_output: bfloat16 [8192, 1024], P('seq', 'head')
The draws below stay inside these ranges and needn't reach their ends.
All inputs are finite; a program needn't handle non-finite values.
Results may differ from the reference program's by a relative error of at most 0.0102.
Values may be sent and summed in bfloat16 or wider, within the bound.
A program may use at most 128 MiB of HBM per device.

```python
import math
import jax
import jax.numpy as jnp
from jax import lax

D = 1024
HEADS = 16
HEAD_DIM = 64
FF = 4096
VOCAB = 256
SHORTEN = 4
WINDOW = 1024
TOKENS = 8192
COARSE = 2048


def draw_token_ids(key, part):
    region = 512
    region_count = TOKENS // region
    subkeys = jax.random.split(key, 5)
    centers = jax.random.randint(subkeys[0], (region_count,), 0, 256)
    spreads = jax.random.randint(subkeys[1], (region_count,), 2, 48)
    raw_noise = jax.random.randint(subkeys[2], (TOKENS,), 0, 65536)
    center_rows = jnp.repeat(centers, region)
    spread_rows = jnp.repeat(spreads, region)
    levels = jnp.clip(center_rows + raw_noise % (2 * spread_rows + 1) - spread_rows, 0, 255)
    lowest = jax.random.randint(subkeys[3], (), 0, TOKENS)
    stride = jax.random.randint(subkeys[4], (), 1, TOKENS)
    highest = (lowest + stride) % TOKENS
    levels = levels.at[lowest].set(0).at[highest].set(255)
    return levels.astype(jnp.int32)


def drawn_pair(key, which):
    base_key = jax.random.fold_in(key, which)
    first_key, second_key = jax.random.split(base_key, 2)
    columns = HEADS * HEAD_DIM
    querying = jax.random.normal(first_key, (D, columns), jnp.float32) * D ** (-0.5)
    keying = jax.random.normal(second_key, (D, columns), jnp.float32) * D ** (-0.5)
    return (jnp.clip(querying, -2.0, 2.0), jnp.clip(keying, -2.0, 2.0))


def draw_fine_query(key, part):
    return drawn_pair(key, 11)[0].astype(jnp.bfloat16)


def draw_fine_key(key, part):
    return drawn_pair(key, 11)[1].astype(jnp.bfloat16)


def draw_coarse_query(key, part):
    return drawn_pair(key, 23)[0].astype(jnp.bfloat16)


def draw_coarse_key(key, part):
    return drawn_pair(key, 23)[1].astype(jnp.bfloat16)


def shard_levels(own_key, shape, cuts, smallest, largest):
    def one(axis_at, parts):
        draws = jax.random.uniform(jax.random.fold_in(jax.random.fold_in(own_key, 6), axis_at), (parts,), jnp.float32, smallest / len(cuts), largest / len(cuts))
        return jnp.repeat(jnp.exp(draws), shape[axis_at] // parts).reshape((-1,) + (1,) * (len(shape) - axis_at - 1))

    level = one(*cuts[0])
    for cut in cuts[1:]:
        level = level * one(*cut)
    return level


def gaussian(key, extent, scale, bound, pieces=(), kind=jnp.bfloat16):
    values = scale * jax.random.normal(key, extent, jnp.float32)
    if pieces:
        values = values * shard_levels(key, extent, pieces, -0.22, 0.18)
    return jnp.clip(values, -bound, bound).astype(kind)


def setup_inputs(seed: int = 0) -> dict:
    seeds = jax.random.split(jax.random.key(seed), 18)
    return {
        "token_ids": draw_token_ids(jax.random.fold_in(seeds[17], 71), 0),
        "embedding": gaussian(seeds[1], (VOCAB, D), 1.0, 6.0),
        "fine_norm": jnp.clip(1.0 + 0.18 * jax.random.normal(seeds[2], (D,), jnp.float32), 0.1, 1.9),
        "fine_query": draw_fine_query(jax.random.fold_in(seeds[17], 71), 0),
        "fine_key": draw_fine_key(jax.random.fold_in(seeds[17], 71), 0),
        "fine_value": gaussian(seeds[5], (D, HEADS * HEAD_DIM), D ** -0.5, 0.1875, ((1, 4),)),
        "fine_output": gaussian(seeds[6], (HEADS * HEAD_DIM, D), (HEADS * HEAD_DIM) ** -0.5, 0.1875, ((0, 4),)),
        "shorten_weight": gaussian(seeds[7], (SHORTEN, D, D), (SHORTEN * D) ** -0.5, 0.09375, ((1, 4),)),
        "coarse_norm": jnp.clip(1.0 + 0.18 * jax.random.normal(seeds[8], (D,), jnp.float32), 0.1, 1.9),
        "coarse_query": draw_coarse_query(jax.random.fold_in(seeds[17], 71), 0),
        "coarse_key": draw_coarse_key(jax.random.fold_in(seeds[17], 71), 0),
        "coarse_value": gaussian(seeds[11], (D, HEADS * HEAD_DIM), D ** -0.5, 0.1875, ((1, 4),)),
        "coarse_output": gaussian(seeds[12], (HEADS * HEAD_DIM, D), (HEADS * HEAD_DIM) ** -0.5, 0.1875, ((0, 4),)),
        "ffn_norm": jnp.clip(1.0 + 0.18 * jax.random.normal(seeds[13], (D,), jnp.float32), 0.1, 1.9),
        "ffn_up": gaussian(seeds[14], (D, FF), D ** -0.5, 0.1875, ((1, 4),)),
        "ffn_down": gaussian(seeds[15], (FF, D), FF ** -0.5, 0.09375, ((0, 4),)),
        "upsample_weight": gaussian(seeds[16], (D, SHORTEN, D), D ** -0.5, 0.1875, ((2, 4),)),
    }


epsilon = 1e-06
masked_low = -1e+30

def rms_scale(values, gain):
    data = values.astype(jnp.float32)
    power = lax.optimization_barrier(jnp.mean(data * data, axis=-1, keepdims=True))
    return (data * lax.rsqrt(power + epsilon) * gain).astype(jnp.bfloat16)

def project(left, right):
    return jnp.dot(left, right, preferred_element_type=jnp.float32)

def rotate(values, positions):
    rows = values.shape[0]
    halfway = HEAD_DIM // 2
    pairs = values.reshape(rows, -1, 2, halfway)
    column_index = jnp.arange(halfway, dtype=jnp.int32)
    periods = 2 ** (4 + column_index * 14 // halfway)
    cycle = (positions[:, None] % periods[None, :]).astype(jnp.float32)
    angle = cycle * (2.0 * math.pi / periods.astype(jnp.float32))[None, :]
    cosine = jnp.cos(angle)[:, None, :]
    sine_part = jnp.sin(angle)[:, None, :]
    lower = pairs[:, :, 0]
    upper = pairs[:, :, 1]
    turned = jnp.stack([lower * cosine - upper * sine_part, upper * cosine + lower * sine_part], axis=2)
    return turned.reshape(rows, -1)

def weighted(scores, allowed, values):
    highest = lax.optimization_barrier(jnp.max(jnp.where(allowed, scores, masked_low), axis=-1, keepdims=True))
    weights = jnp.where(allowed, jnp.exp(scores - highest), 0.0)
    totals = lax.optimization_barrier(jnp.sum(weights, axis=-1))
    rounded = lax.optimization_barrier(weights.astype(jnp.bfloat16))
    mixed = jnp.einsum('hqk,khd->qhd', rounded.astype(jnp.float32), values.astype(jnp.float32))
    return mixed / jnp.transpose(totals)[:, :, None]

def fine_attention(query, keys, values):
    length = query.shape[0]
    block = min(512, length)
    padding = jnp.zeros((WINDOW,) + keys.shape[1:], keys.dtype)
    keys_long = jnp.concatenate([padding, keys])
    values_long = jnp.concatenate([padding, values])
    offsets = jnp.arange(block, dtype=jnp.int32)
    reaches = jnp.arange(block + WINDOW, dtype=jnp.int32)
    scale = HEAD_DIM ** (-0.5)

    def one_block(index):
        begin = index * block
        query_rows = lax.dynamic_slice_in_dim(query, begin, block, 0)
        key_rows = lax.dynamic_slice_in_dim(keys_long, begin, block + WINDOW, 0)
        value_rows = lax.dynamic_slice_in_dim(values_long, begin, block + WINDOW, 0)
        scores = jnp.einsum('qhd,khd->hqk', query_rows.astype(jnp.float32), key_rows.astype(jnp.float32)) * scale
        allowed = (reaches[None, :] > offsets[:, None]) & (reaches[None, :] <= offsets[:, None] + WINDOW) & (begin + reaches[None, :] >= WINDOW)
        return weighted(scores, allowed[None], value_rows)
    mixed = lax.map(one_block, jnp.arange(length // block, dtype=jnp.int32))
    return mixed.reshape(length, -1).astype(jnp.bfloat16)

def coarse_attention(query, keys, values):
    length = query.shape[0]
    block = min(512, length)
    positions = jnp.arange(length, dtype=jnp.int32)
    offsets = jnp.arange(block, dtype=jnp.int32)
    scale = HEAD_DIM ** (-0.5)

    def one_block(index):
        begin = index * block
        query_rows = lax.dynamic_slice_in_dim(query, begin, block, 0)
        scores = jnp.einsum('qhd,khd->hqk', query_rows.astype(jnp.float32), keys.astype(jnp.float32)) * scale
        allowed = positions[None, :] <= begin + offsets[:, None]
        return weighted(scores, allowed[None], values)
    mixed = lax.map(one_block, jnp.arange(length // block, dtype=jnp.int32))
    return mixed.reshape(length, -1).astype(jnp.bfloat16)

def split_heads(values):
    return values.reshape(values.shape[0], HEADS, HEAD_DIM)

def reference(token_ids, embedding, fine_norm, fine_query, fine_key, fine_value, fine_output, shorten_weight, coarse_norm, coarse_query, coarse_key, coarse_value, coarse_output, ffn_norm, ffn_up, ffn_down, upsample_weight):
    fine_pos = jnp.arange(TOKENS, dtype=jnp.int32)
    coarse_pos = jnp.arange(COARSE, dtype=jnp.int32)
    start = embedding[token_ids]
    fine_in = rms_scale(start, fine_norm)
    fine_q = split_heads(rotate(project(fine_in, fine_query), fine_pos).astype(jnp.bfloat16))
    fine_k = split_heads(rotate(project(fine_in, fine_key), fine_pos).astype(jnp.bfloat16))
    fine_v = split_heads(project(fine_in, fine_value).astype(jnp.bfloat16))
    fine_mixed = fine_attention(fine_q, fine_k, fine_v)
    fine = (start.astype(jnp.float32) + project(fine_mixed, fine_output)).astype(jnp.bfloat16)
    padded = jnp.concatenate([jnp.zeros((SHORTEN - 1, D), jnp.bfloat16), fine])
    grouped = jnp.concatenate([padded[offset:offset + TOKENS:SHORTEN] for offset in range(SHORTEN)], axis=1)
    short = project(grouped, shorten_weight.reshape(SHORTEN * D, D)).astype(jnp.bfloat16)
    coarse_in = rms_scale(short, coarse_norm)
    coarse_q = split_heads(rotate(project(coarse_in, coarse_query), coarse_pos).astype(jnp.bfloat16))
    coarse_k = split_heads(rotate(project(coarse_in, coarse_key), coarse_pos).astype(jnp.bfloat16))
    coarse_v = split_heads(project(coarse_in, coarse_value).astype(jnp.bfloat16))
    coarse_mixed = coarse_attention(coarse_q, coarse_k, coarse_v)
    first = short.astype(jnp.float32) + project(coarse_mixed, coarse_output)
    inner = jax.nn.gelu(project(rms_scale(first, ffn_norm), ffn_up)).astype(jnp.bfloat16)
    second = (first + project(inner, ffn_down)).astype(jnp.bfloat16)
    lifted = project(second, upsample_weight.reshape(D, SHORTEN * D)).reshape(TOKENS, D)
    return (fine.astype(jnp.float32) + lifted).astype(jnp.bfloat16)
```

```python
import math

import jax
import jax.numpy as jnp
from jax import lax
from jax.experimental import pallas as pl
from jax.experimental.pallas import tpu as pltpu
from jax.sharding import PartitionSpec as P

D = 1024
HEAD_DIM = 64
SHORTEN = 4
WINDOW = 1024


epsilon = 1e-06
masked_low = -1e30
MESH = pl.DeviceIdType.MESH
EXP2_SCALE = HEAD_DIM ** (-0.5) * math.log2(math.e)
VMEM_SPEC = pl.BlockSpec(memory_space=pltpu.VMEM)
SMEM_SPEC = pl.BlockSpec(memory_space=pltpu.SMEM)


def shifted(value, axis, steps):
    count = lax.axis_size(axis)
    first, last = (max(0, -steps), min(count, count - steps))
    return lax.ppermute(value, axis, [(source, source + steps) for source in range(first, last)])


def project(left, right):
    return jnp.dot(left, right, preferred_element_type=jnp.float32)


def rms_scale(values, gain):
    data = values.astype(jnp.float32)
    power = jnp.mean(data * data, axis=-1, keepdims=True)
    return (data * lax.rsqrt(power + epsilon) * gain).astype(jnp.bfloat16)


def column_periods(width):
    halfway = HEAD_DIM // 2
    column_index = jnp.arange(width, dtype=jnp.int32) % halfway
    return 2 ** (4 + column_index * 14 // halfway)


def angles(positions, width):
    periods = column_periods(width)
    cycle = (positions[:, None] % periods[None, :]).astype(jnp.float32)
    return cycle * (2.0 * math.pi / periods.astype(jnp.float32))[None, :]


def turn_tables(begin, rows, width):
    lanes = min(128, width)
    fine_rows = min(64, rows)
    coarse = angles(begin + fine_rows * jnp.arange(rows // fine_rows, dtype=jnp.int32), lanes)
    small = angles(jnp.arange(fine_rows, dtype=jnp.int32), lanes)
    sign = jnp.where(jnp.arange(lanes) % HEAD_DIM < HEAD_DIM // 2, -1.0, 1.0).astype(jnp.float32)
    cos_a, sin_a = jnp.cos(coarse)[:, None, :], jnp.sin(coarse)[:, None, :]
    cos_b, sin_b = jnp.cos(small)[None], jnp.sin(small)[None]
    cosine = (cos_a * cos_b - sin_a * sin_b).reshape(rows, lanes)
    sine = ((sin_a * cos_b + cos_a * sin_b) * sign).reshape(rows, lanes)
    reps = width // lanes
    return jnp.tile(cosine, (1, reps)), jnp.tile(sine, (1, reps))


def swapped(values):
    halfway = HEAD_DIM // 2
    pieces = []
    for start in range(0, values.shape[1], HEAD_DIM):
        pieces.append(values[:, start + halfway : start + HEAD_DIM])
        pieces.append(values[:, start : start + halfway])
    return jnp.concatenate(pieces, axis=1)


def split_two(values):
    high = lax.reduce_precision(values, 8, 7)
    low = lax.reduce_precision(values - high, 8, 7)
    return high.astype(jnp.bfloat16), low.astype(jnp.bfloat16)


def transposed_dot(left, right):
    return lax.dot_general(
        left, right, (((1,), (1,)), ((), ())), preferred_element_type=jnp.float32
    )


def fine_kernel(place_ref, q_ref, k_ref, v_ref, out_ref):
    rows, width = q_ref.shape
    heads = width // HEAD_DIM
    index = pl.program_id(0)
    begin = pl.multiple_of(index * rows, rows)
    span = WINDOW + rows

    def run(first_device):
        keys = k_ref[pl.ds(begin, span), :]
        values = v_ref[pl.ds(begin, span), :]
        query = q_ref[...]
        lane_head = lax.broadcasted_iota(jnp.int32, (rows, width), 1) // HEAD_DIM
        row = lax.broadcasted_iota(jnp.int32, (rows, rows), 0)
        column = lax.broadcasted_iota(jnp.int32, (rows, rows), 1)
        result = jnp.zeros((rows, width), jnp.float32)
        for head in range(heads):
            masked_q = jnp.where(lane_head == head, query, jnp.zeros_like(query))
            scores = transposed_dot(masked_q, keys)
            pieces = []
            for at in range(0, span, rows):
                piece = scores[:, at : at + rows]
                if at == 0:
                    piece = jnp.where(column > row, piece, masked_low)
                if at == span - rows:
                    piece = jnp.where(column <= row, piece, masked_low)
                elif first_device:
                    piece = jnp.where(begin + at + column >= WINDOW, piece, masked_low)
                pieces.append(piece)
            top = pieces[0]
            for piece in pieces[1:]:
                top = jnp.maximum(top, piece)
            top = jnp.max(top, axis=1, keepdims=True)
            weights = [jnp.exp2((piece - top) * EXP2_SCALE) for piece in pieces]
            total = weights[0]
            for piece in weights[1:]:
                total = total + piece
            total = jnp.sum(total, axis=1, keepdims=True)
            rounded = jnp.concatenate([piece.astype(jnp.bfloat16) for piece in weights], axis=1)
            mixed = jnp.dot(rounded, values, preferred_element_type=jnp.float32)
            result = jnp.where(lane_head == head, mixed / total, result)
        out_ref[...] = result.astype(jnp.bfloat16)

    @pl.when(place_ref[0] == 0)
    def _():
        run(True)

    @pl.when(place_ref[0] != 0)
    def _():
        run(False)


def fine_attention(place, query, keys, values):
    count, width = query.shape
    rows = min(256, count)
    return pl.pallas_call(
        fine_kernel,
        grid=(count // rows,),
        out_shape=jax.ShapeDtypeStruct((count, width), jnp.bfloat16),
        in_specs=[
            SMEM_SPEC,
            pl.BlockSpec((rows, width), lambda i: (i, 0)),
            pl.BlockSpec(keys.shape, lambda i: (0, 0)),
            pl.BlockSpec(values.shape, lambda i: (0, 0)),
        ],
        out_specs=pl.BlockSpec((rows, width), lambda i: (i, 0)),
        compiler_params=pltpu.CompilerParams(vmem_limit_bytes=48 * 2**20),
        cost_estimate=pl.CostEstimate(
            flops=4 * count * (WINDOW + rows) * width,
            bytes_accessed=2 * (2 * query.size + keys.size + values.size),
            transcendentals=count * (WINDOW + rows) * (width // HEAD_DIM),
        ),
        name="fine_attention",
    )(place, query, keys, values)


def coarse_kernel(place_ref, q_ref, kv_ref, out_ref, top_ref, total_ref, acc_ref):
    rows, width = q_ref.shape
    heads = width // HEAD_DIM
    place = place_ref[0]
    lane_head = lax.broadcasted_iota(jnp.int32, (rows, width), 1) // HEAD_DIM
    query = q_ref[...]

    def absorb(block, diagonal):
        keys = kv_ref[block, :, :width]
        values = kv_ref[block, :, width:]
        for head in range(heads):
            masked_q = jnp.where(lane_head == head, query, jnp.zeros_like(query))
            scores = transposed_dot(masked_q, keys)
            if diagonal:
                row = lax.broadcasted_iota(jnp.int32, scores.shape, 0)
                column = lax.broadcasted_iota(jnp.int32, scores.shape, 1)
                scores = jnp.where(column <= row, scores, masked_low)
            peak = jnp.max(scores, axis=1, keepdims=True)
            if diagonal:
                fresh = peak
            else:
                fresh = jnp.maximum(top_ref[head], peak)
            weights = jnp.exp2((scores - fresh) * EXP2_SCALE)
            total = jnp.sum(weights, axis=1, keepdims=True)
            mixed = jnp.dot(weights.astype(jnp.bfloat16), values, preferred_element_type=jnp.float32)
            if not diagonal:
                factor = jnp.exp2((top_ref[head] - fresh) * EXP2_SCALE)
                total = total + total_ref[head] * factor
                mixed = mixed + acc_ref[head] * factor
            top_ref[head] = fresh
            total_ref[head] = total
            acc_ref[head] = mixed

    absorb(place, True)

    def step(block, carry):
        absorb(block, False)
        return carry

    lax.fori_loop(0, place, step, 0)
    result = jnp.zeros((rows, width), jnp.float32)
    for head in range(heads):
        result = jnp.where(lane_head == head, acc_ref[head] / total_ref[head], result)
    out_ref[...] = result.astype(jnp.bfloat16)


def coarse_attention(place, query, gathered):
    rows, width = query.shape
    heads = width // HEAD_DIM
    return pl.pallas_call(
        coarse_kernel,
        out_shape=jax.ShapeDtypeStruct((rows, width), jnp.bfloat16),
        in_specs=[SMEM_SPEC, VMEM_SPEC, VMEM_SPEC],
        out_specs=VMEM_SPEC,
        scratch_shapes=[
            pltpu.VMEM((heads, rows, 1), jnp.float32),
            pltpu.VMEM((heads, rows, 1), jnp.float32),
            pltpu.VMEM((heads, rows, width), jnp.float32),
        ],
        compiler_params=pltpu.CompilerParams(vmem_limit_bytes=48 * 2**20),
        name="coarse_attention",
    )(place, query, gathered)


def head_peers():
    me = lax.axis_index("head")
    sibling = me + 1 - 2 * (me % 2)
    across = (me + 2) % 4
    diagonal = (sibling + 2) % 4
    return me, sibling, across, diagonal


def remote(source, target, send, receive, axis, device):
    return pltpu.make_async_remote_copy(
        src_ref=source,
        dst_ref=target,
        send_sem=send,
        recv_sem=receive,
        device_id={axis: device},
        device_id_type=MESH,
    )


def greet(axis, devices):
    barrier = pltpu.get_barrier_semaphore()
    for device in devices:
        pl.semaphore_signal(barrier, inc=1, device_id={axis: device}, device_id_type=MESH)
    pl.semaphore_wait(barrier, len(devices))


GATHER_CHUNKS = 4


def head_gather_kernel(x_ref, out_ref, own_sem, send_sem, recv_sem):
    me, sibling, across, diagonal = head_peers()
    rows, width = x_ref.shape
    size = rows // GATHER_CHUNKS

    def block(at, chunk):
        return out_ref.at[pl.ds(chunk * size, size), pl.ds(at * width, width)]

    greet("head", (sibling, across))
    to_across, to_sibling, relays = [], [], []
    for chunk in range(GATHER_CHUNKS):
        source = x_ref.at[pl.ds(chunk * size, size), :]
        copy = remote(source, block(2, chunk), send_sem.at[0, chunk], recv_sem.at[0, chunk], "head", across)
        copy.start()
        to_across.append(copy)
    for chunk in range(GATHER_CHUNKS):
        source = x_ref.at[pl.ds(chunk * size, size), :]
        copy = remote(source, block(1, chunk), send_sem.at[1, chunk], recv_sem.at[1, chunk], "head", sibling)
        copy.start()
        to_sibling.append(copy)
    own = pltpu.make_async_copy(x_ref, out_ref.at[:, pl.ds(0, width)], own_sem)
    own.start()
    for chunk in range(GATHER_CHUNKS):
        to_across[chunk].wait_recv()
        copy = remote(block(2, chunk), block(3, chunk), send_sem.at[2, chunk], recv_sem.at[2, chunk], "head", sibling)
        copy.start()
        relays.append(copy)
    own.wait()
    for copy in to_across:
        copy.wait_send()
    for copy in to_sibling + relays:
        copy.wait()


def head_gather(values):
    rows, width = values.shape
    return pl.pallas_call(
        head_gather_kernel,
        out_shape=jax.ShapeDtypeStruct((rows, 4 * width), values.dtype),
        in_specs=[VMEM_SPEC],
        out_specs=VMEM_SPEC,
        scratch_shapes=[
            pltpu.SemaphoreType.DMA,
            pltpu.SemaphoreType.DMA((3, GATHER_CHUNKS)),
            pltpu.SemaphoreType.DMA((3, GATHER_CHUNKS)),
        ],
        compiler_params=pltpu.CompilerParams(collective_id=1, has_side_effects=True),
        name="head_gather",
    )(values)


def head_sum_kernel(with_residual, *refs):
    if with_residual:
        part_ref, residual_ref, out_ref, send_a, recv_a, send_b, recv_b, final, send_sem, recv_sem = refs
    else:
        part_ref, out_ref, send_a, recv_a, send_b, recv_b, final, send_sem, recv_sem = refs
    me, sibling, across, diagonal = head_peers()
    width = final.shape[1]

    def columns(place):
        return pl.ds(pl.multiple_of(place * width, width), width)

    greet("head", (sibling, across))
    first = []
    for slot, place in enumerate((diagonal, sibling)):
        send_a[slot] = part_ref[:, columns(place)].astype(send_a.dtype)
        copy = remote(send_a.at[slot], recv_a.at[slot], send_sem.at[slot], recv_sem.at[slot], "head", sibling)
        copy.start()
        first.append(copy)
    first[0].wait_recv()
    send_b[...] = (part_ref[:, columns(across)] + recv_a[0].astype(jnp.float32)).astype(send_b.dtype)
    second = remote(send_b, recv_b, send_sem.at[2], recv_sem.at[2], "head", across)
    second.start()
    first[1].wait_recv()
    total = part_ref[:, columns(me)] + recv_a[1].astype(jnp.float32)
    if with_residual:
        total = total + residual_ref[:, columns(me)].astype(jnp.float32)
    second.wait_recv()
    total = total + recv_b[...].astype(jnp.float32)
    final[...] = total.astype(final.dtype)
    to_across = remote(final, out_ref.at[:, columns(me)], send_sem.at[3], recv_sem.at[3], "head", across)
    to_across.start()
    to_sibling = remote(final, out_ref.at[:, columns(me)], send_sem.at[4], recv_sem.at[4], "head", sibling)
    to_sibling.start()
    out_ref[:, columns(me)] = final[...]
    to_across.wait_recv()
    relay = remote(
        out_ref.at[:, columns(across)], out_ref.at[:, columns(across)], send_sem.at[5], recv_sem.at[5], "head", sibling
    )
    relay.start()
    for copy in first + [second, to_across]:
        copy.wait_send()
    to_sibling.wait()
    relay.wait()


def head_sum(part, residual, identity):
    rows, full = part.shape
    width = full // 4
    operands = (part,) if residual is None else (part, residual)
    block = (rows, width)

    def body(*refs):
        head_sum_kernel(residual is not None, *refs)

    return pl.pallas_call(
        body,
        out_shape=jax.ShapeDtypeStruct((rows, full), jnp.bfloat16),
        in_specs=[VMEM_SPEC] * len(operands),
        out_specs=VMEM_SPEC,
        scratch_shapes=[
            pltpu.VMEM((2,) + block, jnp.bfloat16),
            pltpu.VMEM((2,) + block, jnp.bfloat16),
            pltpu.VMEM(block, jnp.bfloat16),
            pltpu.VMEM(block, jnp.bfloat16),
            pltpu.VMEM(block, jnp.bfloat16),
            pltpu.SemaphoreType.DMA((6,)),
            pltpu.SemaphoreType.DMA((6,)),
        ],
        compiler_params=pltpu.CompilerParams(collective_id=identity, has_side_effects=True),
        name=f"head_sum_{identity}",
    )(*operands)


def seq_gather_kernel(x_ref, out_ref, own_sem, up_send, up_recv, cross_send, cross_recv):
    count = out_ref.shape[0]
    levels = count // 2
    place = lax.axis_index("seq")
    side = place % 2
    level = place // 2
    cross = place + 1 - 2 * side
    above = (place + 2) % count
    below = (place + count - 2) % count
    has_above = level < levels - 1

    own = pltpu.make_async_copy(x_ref, out_ref.at[place], own_sem)
    own.start()
    greet("seq", (cross, above, below))

    def up(source_level, source):
        at = 2 * source_level + side
        return remote(source, out_ref.at[at], up_send.at[source_level], up_recv.at[source_level], "seq", above)

    def over(source_level, source, source_side):
        at = 2 * source_level + source_side
        return remote(source, out_ref.at[at], cross_send.at[source_level], cross_recv.at[source_level], "seq", cross)

    @pl.when(has_above)
    def _():
        up(level, x_ref).start()

    @pl.when(side == 0)
    def _():
        over(level, x_ref, side).start()

    def pass_on(step, carry):
        source_level = level - 1 - step
        block = out_ref.at[2 * source_level + side]
        up(source_level, block).wait_recv()

        @pl.when(has_above)
        def _():
            up(source_level, block).start()

        over(source_level, block, side).start()
        return carry

    lax.fori_loop(0, level, pass_on, 0)
    own.wait()

    def finish_one(step, carry):
        source_level = level - 1 - step
        block = out_ref.at[2 * source_level + side]

        @pl.when(has_above)
        def _():
            up(source_level, block).wait_send()

        over(source_level, block, side).wait_send()
        other = out_ref.at[2 * source_level + 1 - side]
        over(source_level, other, 1 - side).wait_recv()
        return carry

    @pl.when(has_above)
    def _():
        up(level, x_ref).wait_send()

    @pl.when(side == 0)
    def _():
        over(level, x_ref, side).wait_send()

    @pl.when(side == 1)
    def _():
        over(level, out_ref.at[2 * level], 0).wait_recv()

    lax.fori_loop(0, level, finish_one, 0)


def seq_gather(values):
    count = lax.axis_size("seq")
    return pl.pallas_call(
        seq_gather_kernel,
        out_shape=jax.ShapeDtypeStruct((count,) + values.shape, values.dtype),
        in_specs=[VMEM_SPEC],
        out_specs=VMEM_SPEC,
        scratch_shapes=[pltpu.SemaphoreType.DMA]
        + [pltpu.SemaphoreType.DMA((count // 2,)) for _ in range(4)],
        compiler_params=pltpu.CompilerParams(collective_id=2, has_side_effects=True),
        name="seq_gather",
    )(values)


def local(
    token_ids,
    embedding,
    fine_norm,
    fine_query,
    fine_key,
    fine_value,
    fine_output,
    shorten_weight,
    coarse_norm,
    coarse_query,
    coarse_key,
    coarse_value,
    coarse_output,
    ffn_norm,
    ffn_up,
    ffn_down,
    upsample_weight,
):
    row_count = token_ids.shape[0]
    seq_place = lax.axis_index("seq")
    place = jnp.reshape(seq_place, (1,)).astype(jnp.int32)
    head_count = lax.axis_size("head")
    head_place = lax.axis_index("head")
    share = D // head_count
    column_start = head_place * share
    width = fine_query.shape[1]

    prior_ids = shifted(token_ids, "seq", 1)
    column_parts = [lax.dynamic_slice_in_dim(fine_output, column_start, share, 1)]
    for flip in range(1, head_count):
        piece = lax.dynamic_slice_in_dim(fine_output, (head_place ^ flip) * share, share, 1)
        column_parts.append(
            lax.ppermute(piece, "head", [(source, source ^ flip) for source in range(head_count)])
        )
    column_rows = jnp.concatenate(column_parts)

    level_in = rms_scale(embedding, fine_norm)
    level_q = project(level_in, fine_query)
    level_k = project(level_in, fine_key)
    level_v = project(level_in, fine_value).astype(jnp.bfloat16)
    own_levels = lax.dynamic_slice_in_dim(embedding, column_start, share, 1)
    k_table = jnp.concatenate([*split_two(level_k), *split_two(swapped(level_k)), level_v], axis=1)
    q_table = jnp.concatenate([*split_two(level_q), *split_two(swapped(level_q)), own_levels], axis=1)
    levels = jnp.arange(embedding.shape[0], dtype=jnp.int32)
    both_ids = jnp.concatenate([prior_ids, token_ids])
    one_hot = (both_ids[:, None] == levels[None, :]).astype(jnp.bfloat16)
    cosine, sine = turn_tables((seq_place - 1) * row_count, 2 * row_count, width)

    def rotated(joined, cos_rows, sin_rows):
        plain = joined[:, :width] + joined[:, width : 2 * width]
        other = joined[:, 2 * width : 3 * width] + joined[:, 3 * width : 4 * width]
        return (plain * cos_rows + other * sin_rows).astype(jnp.bfloat16)

    k_rows = project(one_hot, k_table)
    q_rows = project(one_hot[row_count:], q_table)
    fine_k = rotated(k_rows, cosine, sine)
    fine_v = k_rows[:, 4 * width :].astype(jnp.bfloat16)
    fine_q = rotated(q_rows, cosine[row_count:], sine[row_count:])
    own_start = q_rows[:, 4 * width :]
    fine_mixed = fine_attention(place, fine_q, fine_k, fine_v)

    merged = project(head_gather(fine_mixed), column_rows)
    fine = (own_start + merged).astype(jnp.bfloat16)
    carried = shifted(fine[row_count - (SHORTEN - 1) :], "seq", 1)
    padded = jnp.concatenate([carried, fine])
    grouped = jnp.concatenate(
        [padded[offset : offset + row_count : SHORTEN] for offset in range(SHORTEN)], axis=1
    )
    short = head_sum(project(grouped, shorten_weight.reshape(SHORTEN * share, D)), None, 3)

    coarse_rows = row_count // SHORTEN
    coarse_in = rms_scale(short, coarse_norm)
    cosine, sine = turn_tables(seq_place * coarse_rows, coarse_rows, width)

    def turned(values):
        return (values * cosine + swapped(values) * sine).astype(jnp.bfloat16)

    coarse_q = turned(project(coarse_in, coarse_query))
    coarse_k = turned(project(coarse_in, coarse_key))
    coarse_v = project(coarse_in, coarse_value).astype(jnp.bfloat16)
    gathered = seq_gather(jnp.concatenate([coarse_k, coarse_v], axis=1))
    coarse_mixed = coarse_attention(place, coarse_q, gathered)
    first = short.astype(jnp.float32) + head_sum(
        project(coarse_mixed, coarse_output), None, 4
    ).astype(jnp.float32)
    inner = jax.nn.gelu(project(rms_scale(first, ffn_norm), ffn_up)).astype(jnp.bfloat16)
    second = head_sum(project(inner, ffn_down), first, 5)
    lifted = project(second, upsample_weight.reshape(D, SHORTEN * share)).reshape(row_count, share)
    return (fine.astype(jnp.float32) + lifted).astype(jnp.bfloat16)


def solution(mesh):
    return jax.shard_map(
        local,
        mesh=mesh,
        in_specs=(
            P("seq"),
            P(),
            P(),
            P(None, "head"),
            P(None, "head"),
            P(None, "head"),
            P("head", None),
            P(None, "head", None),
            P(),
            P(None, "head"),
            P(None, "head"),
            P(None, "head"),
            P("head", None),
            P(),
            P(None, "head"),
            P("head", None),
            P(None, None, "head"),
        ),
        out_specs=P("seq", "head"),
        check_vma=False,
    )
```

```python
import math

import jax
import jax.numpy as jnp
from jax import lax
from jax.experimental import pallas as pl
from jax.experimental.pallas import tpu as pltpu
from jax.sharding import PartitionSpec as P

D = 1024
HEAD_DIM = 64
SHORTEN = 4
WINDOW = 1024


epsilon = 1e-06
masked_low = -1e30
MESH = pl.DeviceIdType.MESH
EXP2_SCALE = HEAD_DIM ** (-0.5) * math.log2(math.e)
VMEM_SPEC = pl.BlockSpec(memory_space=pltpu.VMEM)


def shifted(value, axis, steps):
    count = lax.axis_size(axis)
    first, last = (max(0, -steps), min(count, count - steps))
    return lax.ppermute(value, axis, [(source, source + steps) for source in range(first, last)])


def project(left, right):
    return jnp.dot(left, right, preferred_element_type=jnp.float32)


def rms_scale(values, gain):
    data = values.astype(jnp.float32)
    power = jnp.mean(data * data, axis=-1, keepdims=True)
    return (data * lax.rsqrt(power + epsilon) * gain).astype(jnp.bfloat16)


def column_periods(width):
    halfway = HEAD_DIM // 2
    column_index = jnp.arange(width, dtype=jnp.int32) % halfway
    return 2 ** (4 + column_index * 14 // halfway)


def angles(positions, width):
    periods = column_periods(width)
    cycle = (positions[:, None] % periods[None, :]).astype(jnp.float32)
    return cycle * (2.0 * math.pi / periods.astype(jnp.float32))[None, :]


def turn_tables(begin, rows, width):
    lanes = min(128, width)
    fine_rows = min(64, rows)
    coarse = angles(begin + fine_rows * jnp.arange(rows // fine_rows, dtype=jnp.int32), lanes)
    small = angles(jnp.arange(fine_rows, dtype=jnp.int32), lanes)
    sign = jnp.where(jnp.arange(lanes) % HEAD_DIM < HEAD_DIM // 2, -1.0, 1.0).astype(jnp.float32)
    cos_a, sin_a = jnp.cos(coarse)[:, None, :], jnp.sin(coarse)[:, None, :]
    cos_b, sin_b = jnp.cos(small)[None], jnp.sin(small)[None]
    cosine = (cos_a * cos_b - sin_a * sin_b).reshape(rows, lanes)
    sine = ((sin_a * cos_b + cos_a * sin_b) * sign).reshape(rows, lanes)
    reps = width // lanes
    return jnp.tile(cosine, (1, reps)), jnp.tile(sine, (1, reps))


def swapped(values):
    halfway = HEAD_DIM // 2
    pieces = []
    for start in range(0, values.shape[1], HEAD_DIM):
        pieces.append(values[:, start + halfway : start + HEAD_DIM])
        pieces.append(values[:, start : start + halfway])
    return jnp.concatenate(pieces, axis=1)


def split_two(values):
    high = lax.reduce_precision(values, 8, 7)
    low = lax.reduce_precision(values - high, 8, 7)
    return high.astype(jnp.bfloat16), low.astype(jnp.bfloat16)


def transposed_dot(left, right):
    return lax.dot_general(
        left, right, (((1,), (1,)), ((), ())), preferred_element_type=jnp.float32
    )


def head_peers():
    me = lax.axis_index("head")
    sibling = me + 1 - 2 * (me % 2)
    across = (me + 2) % 4
    diagonal = (sibling + 2) % 4
    return me, sibling, across, diagonal


def remote(source, target, send, receive, axis, device):
    return pltpu.make_async_remote_copy(
        src_ref=source,
        dst_ref=target,
        send_sem=send,
        recv_sem=receive,
        device_id={axis: device},
        device_id_type=MESH,
    )


def greet(axis, devices):
    barrier = pltpu.get_barrier_semaphore()
    for device in devices:
        pl.semaphore_signal(barrier, inc=1, device_id={axis: device}, device_id_type=MESH)
    pl.semaphore_wait(barrier, len(devices))


CARRY_ROWS = 16


def fine_kernel(
    q_ref, k_ref, v_ref, start_ref, cols_ref, w_ref, part_ref, fine_ref,
    mixed, others, carry, stream, send_sem, recv_sem, carry_send, carry_recv,
):
    count, width = q_ref.shape
    rows = min(256, count)
    chunks = count // rows
    heads = width // HEAD_DIM
    span = WINDOW + rows
    seq_count = lax.axis_size("seq")
    place = lax.axis_index("seq")
    me, sibling, across, diagonal = head_peers()
    after = (place + 1) % seq_count
    before = (place + seq_count - 1) % seq_count
    has_next = place < seq_count - 1

    barrier = pltpu.get_barrier_semaphore()
    for device in (sibling, across):
        pl.semaphore_signal(barrier, inc=1, device_id={"head": device}, device_id_type=MESH)
    for line in (after, before):
        for device in range(4):
            pl.semaphore_signal(
                barrier, inc=1, device_id={"seq": line, "head": device}, device_id_type=MESH
            )
    pl.semaphore_wait(barrier, 10)

    def at_rows(chunk):
        return pl.ds(pl.multiple_of(chunk * rows, rows), rows)

    def slot(at, chunk):
        return others.at[at_rows(chunk), pl.ds((at - 1) * width, width)]

    def to_across(chunk):
        return remote(mixed.at[at_rows(chunk), :], slot(2, chunk), send_sem.at[0, chunk], recv_sem.at[0, chunk], "head", across)

    def to_sibling(chunk):
        return remote(mixed.at[at_rows(chunk), :], slot(1, chunk), send_sem.at[1, chunk], recv_sem.at[1, chunk], "head", sibling)

    def relay(chunk):
        return remote(slot(2, chunk), slot(3, chunk), send_sem.at[2, chunk], recv_sem.at[2, chunk], "head", sibling)

    def carry_copy(flip, device):
        return pltpu.make_async_remote_copy(
            src_ref=mixed.at[pl.ds(count - CARRY_ROWS, CARRY_ROWS), :],
            dst_ref=carry.at[:, pl.ds(flip * width, width)],
            send_sem=carry_send.at[flip],
            recv_sem=carry_recv.at[flip],
            device_id={"seq": after, "head": device},
            device_id_type=MESH,
        )

    carries = [carry_copy(flip, device) for flip, device in enumerate((me, sibling, across, diagonal))]
    lane_head = lax.broadcasted_iota(jnp.int32, (rows, width), 1) // HEAD_DIM
    row = lax.broadcasted_iota(jnp.int32, (rows, rows), 0)
    column = lax.broadcasted_iota(jnp.int32, (rows, rows), 1)

    def attend(chunk):
        begin = pl.multiple_of(chunk * rows, rows)
        keys = k_ref[pl.ds(begin, span), :]
        values = v_ref[pl.ds(begin, span), :]
        query = q_ref[at_rows(chunk), :]
        floor = jnp.where(place == 0, WINDOW - begin, 0)
        result = jnp.zeros((rows, width), jnp.float32)
        for head in range(heads):
            masked_q = jnp.where(lane_head == head, query, jnp.zeros_like(query))
            scores = transposed_dot(masked_q, keys)
            pieces = []
            for at in range(0, span, rows):
                piece = scores[:, at : at + rows]
                if at == span - rows:
                    allowed = column <= row
                else:
                    allowed = column >= floor - at
                    if at == 0:
                        allowed = allowed & (column > row)
                pieces.append(jnp.where(allowed, piece, masked_low))
            top = pieces[0]
            for piece in pieces[1:]:
                top = jnp.maximum(top, piece)
            top = jnp.max(top, axis=1, keepdims=True)
            weights = [jnp.exp2((piece - top) * EXP2_SCALE) for piece in pieces]
            total = weights[0]
            for piece in weights[1:]:
                total = total + piece
            total = jnp.sum(total, axis=1, keepdims=True)
            rounded = jnp.concatenate([piece.astype(jnp.bfloat16) for piece in weights], axis=1)
            out = jnp.dot(rounded, values, preferred_element_type=jnp.float32)
            result = jnp.where(lane_head == head, out / total, result)
        mixed[at_rows(chunk), :] = result.astype(jnp.bfloat16)

    def one_chunk(chunk, state):
        attend(chunk)
        to_across(chunk).start()
        to_sibling(chunk).start()

        @pl.when(chunk > 0)
        def _():
            to_across(chunk - 1).wait_recv()
            relay(chunk - 1).start()

        return state

    lax.fori_loop(0, chunks, one_chunk, 0)

    @pl.when(has_next)
    def _():
        for copy in carries:
            copy.start()

    to_across(chunks - 1).wait_recv()
    relay(chunks - 1).start()

    def finish_chunk(chunk, state):
        to_sibling(chunk).wait_recv()
        relay(chunk).wait_recv()
        merged = jnp.dot(mixed[at_rows(chunk), :], cols_ref[:width, :], preferred_element_type=jnp.float32)
        merged = merged + jnp.dot(others[at_rows(chunk), :], cols_ref[width:, :], preferred_element_type=jnp.float32)
        begin = pl.multiple_of(CARRY_ROWS + chunk * rows, CARRY_ROWS)
        value = (start_ref[pl.ds(begin, rows), :].astype(jnp.float32) + merged).astype(jnp.bfloat16)
        fine_ref[at_rows(chunk), :] = value
        for lane in range(width // 128):
            stream[lane, pl.ds(begin, rows), :] = value[:, lane * 128 : lane * 128 + 128].astype(jnp.float32)
        return state

    lax.fori_loop(0, chunks, finish_chunk, 0)

    @pl.when(place == 0)
    def _():
        stream[:, 0:CARRY_ROWS, :] = jnp.zeros((width // 128, CARRY_ROWS, 128), jnp.float32)

    @pl.when(place > 0)
    def _():
        for copy in carries:
            copy.wait_recv()
        merged = jnp.dot(carry[...], cols_ref[...], preferred_element_type=jnp.float32)
        value = (start_ref[0:CARRY_ROWS, :].astype(jnp.float32) + merged).astype(jnp.bfloat16)
        for lane in range(width // 128):
            stream[lane, 0:CARRY_ROWS, :] = value[:, lane * 128 : lane * 128 + 128].astype(jnp.float32)

    groups = count // SHORTEN
    total = jnp.zeros((groups, w_ref.shape[2]), jnp.float32)
    for offset in range(SHORTEN):
        begin = CARRY_ROWS - (SHORTEN - 1) + offset
        member = jnp.concatenate(
            [stream[lane, pl.ds(begin, groups, stride=SHORTEN), :] for lane in range(width // 128)], axis=1
        )
        total = total + jnp.dot(member.astype(jnp.bfloat16), w_ref[offset], preferred_element_type=jnp.float32)
    part_ref[...] = total

    def drain(chunk, state):
        to_across(chunk).wait_send()
        to_sibling(chunk).wait_send()
        relay(chunk).wait_send()
        return state

    lax.fori_loop(0, chunks, drain, 0)

    @pl.when(has_next)
    def _():
        for copy in carries:
            copy.wait_send()


def fine_stage(query, keys, values, start, columns, weights):
    count, width = query.shape
    chunks = count // min(256, count)
    return pl.pallas_call(
        fine_kernel,
        out_shape=(
            jax.ShapeDtypeStruct((count // SHORTEN, weights.shape[2]), jnp.float32),
            jax.ShapeDtypeStruct((count, width), jnp.bfloat16),
        ),
        in_specs=[VMEM_SPEC] * 6,
        out_specs=(VMEM_SPEC, VMEM_SPEC),
        scratch_shapes=[
            pltpu.VMEM((count, width), jnp.bfloat16),
            pltpu.VMEM((count, 3 * width), jnp.bfloat16),
            pltpu.VMEM((CARRY_ROWS, 4 * width), jnp.bfloat16),
            pltpu.VMEM((width // 128, CARRY_ROWS + count, 128), jnp.float32),
            pltpu.SemaphoreType.DMA((3, chunks)),
            pltpu.SemaphoreType.DMA((3, chunks)),
            pltpu.SemaphoreType.DMA((4,)),
            pltpu.SemaphoreType.DMA((4,)),
        ],
        compiler_params=pltpu.CompilerParams(
            collective_id=1, has_side_effects=True, vmem_limit_bytes=48 * 2**20
        ),
        name="fine_stage",
    )(query, keys, values, start, columns, weights)


def head_sum_kernel(with_residual, *refs):
    if with_residual:
        part_ref, residual_ref, out_ref, send_a, recv_a, send_b, recv_b, final, send_sem, recv_sem = refs
    else:
        part_ref, out_ref, send_a, recv_a, send_b, recv_b, final, send_sem, recv_sem = refs
    me, sibling, across, diagonal = head_peers()
    width = final.shape[1]

    def columns(place):
        return pl.ds(pl.multiple_of(place * width, width), width)

    greet("head", (sibling, across))
    first = []
    for slot, place in enumerate((diagonal, sibling)):
        send_a[slot] = part_ref[:, columns(place)].astype(send_a.dtype)
        copy = remote(send_a.at[slot], recv_a.at[slot], send_sem.at[slot], recv_sem.at[slot], "head", sibling)
        copy.start()
        first.append(copy)
    first[0].wait_recv()
    send_b[...] = (part_ref[:, columns(across)] + recv_a[0].astype(jnp.float32)).astype(send_b.dtype)
    second = remote(send_b, recv_b, send_sem.at[2], recv_sem.at[2], "head", across)
    second.start()
    first[1].wait_recv()
    total = part_ref[:, columns(me)] + recv_a[1].astype(jnp.float32)
    if with_residual:
        total = total + residual_ref[:, columns(me)].astype(jnp.float32)
    second.wait_recv()
    total = total + recv_b[...].astype(jnp.float32)
    final[...] = total.astype(final.dtype)
    to_across = remote(final, out_ref.at[:, columns(me)], send_sem.at[3], recv_sem.at[3], "head", across)
    to_across.start()
    to_sibling = remote(final, out_ref.at[:, columns(me)], send_sem.at[4], recv_sem.at[4], "head", sibling)
    to_sibling.start()
    out_ref[:, columns(me)] = final[...]
    to_across.wait_recv()
    relay = remote(
        out_ref.at[:, columns(across)], out_ref.at[:, columns(across)], send_sem.at[5], recv_sem.at[5], "head", sibling
    )
    relay.start()
    for copy in first + [second, to_across]:
        copy.wait_send()
    to_sibling.wait()
    relay.wait()


def head_sum(part, residual, identity):
    rows, full = part.shape
    width = full // 4
    operands = (part,) if residual is None else (part, residual)
    block = (rows, width)

    def body(*refs):
        head_sum_kernel(residual is not None, *refs)

    return pl.pallas_call(
        body,
        out_shape=jax.ShapeDtypeStruct((rows, full), jnp.bfloat16),
        in_specs=[VMEM_SPEC] * len(operands),
        out_specs=VMEM_SPEC,
        scratch_shapes=[
            pltpu.VMEM((2,) + block, jnp.bfloat16),
            pltpu.VMEM((2,) + block, jnp.bfloat16),
            pltpu.VMEM(block, jnp.bfloat16),
            pltpu.VMEM(block, jnp.bfloat16),
            pltpu.VMEM(block, jnp.bfloat16),
            pltpu.SemaphoreType.DMA((6,)),
            pltpu.SemaphoreType.DMA((6,)),
        ],
        compiler_params=pltpu.CompilerParams(collective_id=identity, has_side_effects=True),
        name=f"head_sum_{identity}",
    )(*operands)


def coarse_kernel(
    short_ref, gain_ref, wq_ref, wk_ref, wv_ref, wo_ref, part_ref,
    pairs, queries, top_ref, total_ref, acc_ref, up_send, up_recv, cross_send, cross_recv,
):
    count, rows, both = pairs.shape
    width = both // 2
    heads = width // HEAD_DIM
    levels = count // 2
    place = lax.axis_index("seq")
    side = place % 2
    level = place // 2
    cross = place + 1 - 2 * side
    above = (place + 2) % count
    below = (place + count - 2) % count
    has_above = level < levels - 1

    lanes = min(128, width)
    lane = lax.broadcasted_iota(jnp.int32, (rows, lanes), 1) % HEAD_DIM
    half_lane = lane % (HEAD_DIM // 2)
    period_log = 4 + (half_lane * 14) // (HEAD_DIM // 2)
    period = jnp.left_shift(jnp.ones_like(period_log), period_log)
    position = place * rows + lax.broadcasted_iota(jnp.int32, (rows, lanes), 0)
    cycle = jnp.bitwise_and(position, period - 1).astype(jnp.float32)
    angle = cycle * (2.0 * math.pi / period.astype(jnp.float32))
    reps = width // lanes
    cosine = jnp.concatenate([jnp.cos(angle)] * reps, axis=1)
    signed = jnp.where(lane < HEAD_DIM // 2, -jnp.sin(angle), jnp.sin(angle))
    sine = jnp.concatenate([signed] * reps, axis=1)
    is_lower = lax.broadcasted_iota(jnp.int32, (rows, width), 1) % HEAD_DIM < HEAD_DIM // 2

    def turned(values):
        other = jnp.where(
            is_lower,
            pltpu.roll(values, width - HEAD_DIM // 2, 1),
            pltpu.roll(values, HEAD_DIM // 2, 1),
        )
        return (values * cosine + other * sine).astype(jnp.bfloat16)

    data = short_ref[...].astype(jnp.float32)
    power = jnp.mean(data * data, axis=1, keepdims=True)
    coarse_in = (data * lax.rsqrt(power + epsilon) * gain_ref[...]).astype(jnp.bfloat16)
    own = pairs.at[place]
    own[:, :width] = turned(jnp.dot(coarse_in, wk_ref[...], preferred_element_type=jnp.float32))
    own[:, width:] = jnp.dot(coarse_in, wv_ref[...], preferred_element_type=jnp.float32).astype(jnp.bfloat16)

    greet("seq", (cross, above, below))

    def up(source_level):
        block = pairs.at[2 * source_level + side]
        return remote(block, block, up_send.at[source_level], up_recv.at[source_level], "seq", above)

    def over(source_level, source_side):
        block = pairs.at[2 * source_level + source_side]
        return remote(block, block, cross_send.at[source_level], cross_recv.at[source_level], "seq", cross)

    @pl.when(has_above)
    def _():
        up(level).start()

    @pl.when(side == 0)
    def _():
        over(level, 0).start()

    query = turned(jnp.dot(coarse_in, wq_ref[...], preferred_element_type=jnp.float32))
    lane_head = lax.broadcasted_iota(jnp.int32, (rows, width), 1) // HEAD_DIM
    for head in range(heads):
        queries[head * rows : (head + 1) * rows, :] = jnp.where(
            lane_head == head, query, jnp.zeros_like(query)
        )

    def absorb(block, diagonal):
        keys = pairs[block, :, :width]
        values = pairs[block, :, width:]
        for head in range(heads):
            part = slice(head * rows, (head + 1) * rows)
            scores = transposed_dot(queries[part, :], keys)
            if diagonal:
                row = lax.broadcasted_iota(jnp.int32, scores.shape, 0)
                column = lax.broadcasted_iota(jnp.int32, scores.shape, 1)
                scores = jnp.where(column <= row, scores, masked_low)
            fresh = jnp.max(scores, axis=1, keepdims=True)
            if not diagonal:
                fresh = jnp.maximum(top_ref[part, :], fresh)
            weights = jnp.exp2((scores - fresh) * EXP2_SCALE)
            total = jnp.sum(weights, axis=1, keepdims=True)
            mixed = jnp.dot(weights.astype(jnp.bfloat16), values, preferred_element_type=jnp.float32)
            if not diagonal:
                factor = jnp.exp2((top_ref[part, :] - fresh) * EXP2_SCALE)
                total = total + total_ref[part, :] * factor
                mixed = mixed + acc_ref[part, :] * factor
            top_ref[part, :] = fresh
            total_ref[part, :] = total
            acc_ref[part, :] = mixed

    absorb(place, True)

    def take_over(source_level):
        over(source_level, 1 - side).wait_recv()
        absorb(2 * source_level + 1 - side, False)

    def one_level(step, state):
        source_level = level - 1 - step
        up(source_level).wait_recv()

        @pl.when(has_above)
        def _():
            up(source_level).start()

        over(source_level, side).start()
        absorb(2 * source_level + side, False)

        @pl.when((step > 0) | (side == 1))
        def _():
            take_over(source_level + 1)

        return state

    lax.fori_loop(0, level, one_level, 0)

    @pl.when((level > 0) | (side == 1))
    def _():
        take_over(0)

    result = jnp.zeros((rows, width), jnp.float32)
    for head in range(heads):
        part = slice(head * rows, (head + 1) * rows)
        result = jnp.where(lane_head == head, acc_ref[part, :] / total_ref[part, :], result)
    part_ref[...] = jnp.dot(result.astype(jnp.bfloat16), wo_ref[...], preferred_element_type=jnp.float32)

    def drain(step, state):
        source_level = level - 1 - step

        @pl.when(has_above)
        def _():
            up(source_level).wait_send()

        over(source_level, side).wait_send()
        return state

    lax.fori_loop(0, level, drain, 0)

    @pl.when(has_above)
    def _():
        up(level).wait_send()

    @pl.when(side == 0)
    def _():
        over(level, 0).wait_send()


def coarse_stage(short, gain, wq, wk, wv, wo):
    rows = short.shape[0]
    width = wq.shape[1]
    heads = width // HEAD_DIM
    count = lax.axis_size("seq")
    return pl.pallas_call(
        coarse_kernel,
        out_shape=jax.ShapeDtypeStruct(short.shape, jnp.float32),
        in_specs=[VMEM_SPEC] * 6,
        out_specs=VMEM_SPEC,
        scratch_shapes=[
            pltpu.VMEM((count, rows, 2 * width), jnp.bfloat16),
            pltpu.VMEM((heads * rows, width), jnp.bfloat16),
            pltpu.VMEM((heads * rows, 1), jnp.float32),
            pltpu.VMEM((heads * rows, 1), jnp.float32),
            pltpu.VMEM((heads * rows, width), jnp.float32),
        ]
        + [pltpu.SemaphoreType.DMA((count // 2,)) for _ in range(4)],
        compiler_params=pltpu.CompilerParams(
            collective_id=2, has_side_effects=True, vmem_limit_bytes=48 * 2**20
        ),
        name="coarse_stage",
    )(short, gain, wq, wk, wv, wo)


def lift_kernel(second_ref, w_ref, fine_ref, out_ref, spread):
    groups = second_ref.shape[0]
    width = fine_ref.shape[1]
    for member in range(SHORTEN):
        lifted = jnp.dot(
            second_ref[...], w_ref[:, member * width : (member + 1) * width], preferred_element_type=jnp.float32
        )
        for lane in range(width // 128):
            spread[lane, pl.ds(member, groups, stride=SHORTEN), :] = lifted[:, lane * 128 : lane * 128 + 128]
    for lane in range(width // 128):
        part = slice(lane * 128, lane * 128 + 128)
        out_ref[:, part] = (fine_ref[:, part].astype(jnp.float32) + spread[lane]).astype(jnp.bfloat16)


def lift_stage(second, weights, fine):
    return pl.pallas_call(
        lift_kernel,
        out_shape=jax.ShapeDtypeStruct(fine.shape, fine.dtype),
        in_specs=[VMEM_SPEC] * 3,
        out_specs=VMEM_SPEC,
        scratch_shapes=[pltpu.VMEM((fine.shape[1] // 128, fine.shape[0], 128), jnp.float32)],
        compiler_params=pltpu.CompilerParams(vmem_limit_bytes=48 * 2**20),
        name="lift_stage",
    )(second, weights, fine)


def local(
    token_ids,
    embedding,
    fine_norm,
    fine_query,
    fine_key,
    fine_value,
    fine_output,
    shorten_weight,
    coarse_norm,
    coarse_query,
    coarse_key,
    coarse_value,
    coarse_output,
    ffn_norm,
    ffn_up,
    ffn_down,
    upsample_weight,
):
    row_count = token_ids.shape[0]
    seq_place = lax.axis_index("seq")
    head_count = lax.axis_size("head")
    head_place = lax.axis_index("head")
    share = D // head_count
    column_start = head_place * share
    width = fine_query.shape[1]

    prior_ids = shifted(token_ids, "seq", 1)
    column_parts = [lax.dynamic_slice_in_dim(fine_output, column_start, share, 1)]
    for flip in range(1, head_count):
        piece = lax.dynamic_slice_in_dim(fine_output, (head_place ^ flip) * share, share, 1)
        column_parts.append(
            lax.ppermute(piece, "head", [(source, source ^ flip) for source in range(head_count)])
        )
    column_rows = jnp.concatenate(column_parts)

    level_in = rms_scale(embedding, fine_norm)
    level_q = project(level_in, fine_query)
    level_k = project(level_in, fine_key)
    level_v = project(level_in, fine_value).astype(jnp.bfloat16)
    own_levels = lax.dynamic_slice_in_dim(embedding, column_start, share, 1)
    k_table = jnp.concatenate([*split_two(level_k), *split_two(swapped(level_k)), level_v], axis=1)
    q_table = jnp.concatenate([*split_two(level_q), *split_two(swapped(level_q)), own_levels], axis=1)
    levels = jnp.arange(embedding.shape[0], dtype=jnp.int32)
    both_ids = jnp.concatenate([prior_ids, token_ids])
    one_hot = (both_ids[:, None] == levels[None, :]).astype(jnp.bfloat16)
    cosine, sine = turn_tables((seq_place - 1) * row_count, 2 * row_count, width)

    def rotated(joined, cos_rows, sin_rows):
        plain = joined[:, :width] + joined[:, width : 2 * width]
        other = joined[:, 2 * width : 3 * width] + joined[:, 3 * width : 4 * width]
        return (plain * cos_rows + other * sin_rows).astype(jnp.bfloat16)

    k_rows = project(one_hot, k_table)
    q_rows = project(one_hot[row_count - CARRY_ROWS :], q_table)
    fine_k = rotated(k_rows, cosine, sine)
    fine_v = k_rows[:, 4 * width :].astype(jnp.bfloat16)
    fine_q = rotated(q_rows[CARRY_ROWS:], cosine[row_count:], sine[row_count:])
    own_start = q_rows[:, 4 * width :].astype(jnp.bfloat16)
    short_part, fine = fine_stage(fine_q, fine_k, fine_v, own_start, column_rows, shorten_weight)
    short = head_sum(short_part, None, 3)
    part = coarse_stage(
        short, coarse_norm.reshape(1, D), coarse_query, coarse_key, coarse_value, coarse_output
    )
    first = short.astype(jnp.float32) + head_sum(part, None, 4).astype(jnp.float32)
    inner = jax.nn.gelu(project(rms_scale(first, ffn_norm), ffn_up)).astype(jnp.bfloat16)
    second = head_sum(project(inner, ffn_down), first, 5)
    return lift_stage(second, upsample_weight.reshape(D, SHORTEN * share), fine)


def solution(mesh):
    return jax.shard_map(
        local,
        mesh=mesh,
        in_specs=(
            P("seq"),
            P(),
            P(),
            P(None, "head"),
            P(None, "head"),
            P(None, "head"),
            P("head", None),
            P(None, "head", None),
            P(),
            P(None, "head"),
            P(None, "head"),
            P(None, "head"),
            P("head", None),
            P(),
            P(None, "head"),
            P("head", None),
            P(None, None, "head"),
        ),
        out_specs=P("seq", "head"),
        check_vma=False,
    )
```

```python
import math

import jax
import jax.numpy as jnp
from jax import lax
from jax.experimental import pallas as pl
from jax.experimental.pallas import tpu as pltpu
from jax.sharding import PartitionSpec as P

D = 1024
HEAD_DIM = 64
SHORTEN = 4
WINDOW = 1024


epsilon = 1e-06
masked_low = -1e30
MESH = pl.DeviceIdType.MESH
EXP2_SCALE = HEAD_DIM ** (-0.5) * math.log2(math.e)
VMEM_SPEC = pl.BlockSpec(memory_space=pltpu.VMEM)


def shifted(value, axis, steps):
    count = lax.axis_size(axis)
    first, last = (max(0, -steps), min(count, count - steps))
    return lax.ppermute(value, axis, [(source, source + steps) for source in range(first, last)])


def project(left, right):
    return jnp.dot(left, right, preferred_element_type=jnp.float32)


def rms_scale(values, gain):
    data = values.astype(jnp.float32)
    power = jnp.mean(data * data, axis=-1, keepdims=True)
    return (data * lax.rsqrt(power + epsilon) * gain).astype(jnp.bfloat16)


def column_periods(width):
    halfway = HEAD_DIM // 2
    column_index = jnp.arange(width, dtype=jnp.int32) % halfway
    return 2 ** (4 + column_index * 14 // halfway)


def angles(positions, width):
    periods = column_periods(width)
    cycle = (positions[:, None] % periods[None, :]).astype(jnp.float32)
    return cycle * (2.0 * math.pi / periods.astype(jnp.float32))[None, :]


def turn_tables(begin, rows, width):
    lanes = min(128, width)
    fine_rows = min(64, rows)
    coarse = angles(begin + fine_rows * jnp.arange(rows // fine_rows, dtype=jnp.int32), lanes)
    small = angles(jnp.arange(fine_rows, dtype=jnp.int32), lanes)
    sign = jnp.where(jnp.arange(lanes) % HEAD_DIM < HEAD_DIM // 2, -1.0, 1.0).astype(jnp.float32)
    cos_a, sin_a = jnp.cos(coarse)[:, None, :], jnp.sin(coarse)[:, None, :]
    cos_b, sin_b = jnp.cos(small)[None], jnp.sin(small)[None]
    cosine = (cos_a * cos_b - sin_a * sin_b).reshape(rows, lanes)
    sine = ((sin_a * cos_b + cos_a * sin_b) * sign).reshape(rows, lanes)
    reps = width // lanes
    return jnp.tile(cosine, (1, reps)), jnp.tile(sine, (1, reps))


def swapped(values):
    halfway = HEAD_DIM // 2
    pieces = []
    for start in range(0, values.shape[1], HEAD_DIM):
        pieces.append(values[:, start + halfway : start + HEAD_DIM])
        pieces.append(values[:, start : start + halfway])
    return jnp.concatenate(pieces, axis=1)


def split_two(values):
    high = lax.reduce_precision(values, 8, 7)
    low = lax.reduce_precision(values - high, 8, 7)
    return high.astype(jnp.bfloat16), low.astype(jnp.bfloat16)


def transposed_dot(left, right):
    return lax.dot_general(
        left, right, (((1,), (1,)), ((), ())), preferred_element_type=jnp.float32
    )


def head_peers():
    me = lax.axis_index("head")
    sibling = me + 1 - 2 * (me % 2)
    across = (me + 2) % 4
    diagonal = (sibling + 2) % 4
    return me, sibling, across, diagonal


def remote(source, target, send, receive, axis, device):
    return pltpu.make_async_remote_copy(
        src_ref=source,
        dst_ref=target,
        send_sem=send,
        recv_sem=receive,
        device_id={axis: device},
        device_id_type=MESH,
    )


CARRY_ROWS = 16


def fine_kernel(
    q_ref, k_ref, v_ref, start_ref, cols_ref, w_ref, part_ref, fine_ref,
    mixed, others, carry, stream, send_sem, recv_sem, carry_send, carry_recv,
):
    count, width = q_ref.shape
    rows = min(256, count)
    chunks = count // rows
    heads = width // HEAD_DIM
    span = WINDOW + rows
    seq_count = lax.axis_size("seq")
    place = lax.axis_index("seq")
    me, sibling, across, diagonal = head_peers()
    after = (place + 1) % seq_count
    before = (place + seq_count - 1) % seq_count
    has_next = place < seq_count - 1

    barrier = pltpu.get_barrier_semaphore()
    for device in (sibling, across):
        pl.semaphore_signal(barrier, inc=1, device_id={"head": device}, device_id_type=MESH)
    for line in (after, before):
        for device in range(4):
            pl.semaphore_signal(
                barrier, inc=1, device_id={"seq": line, "head": device}, device_id_type=MESH
            )
    pl.semaphore_wait(barrier, 10)

    def at_rows(chunk):
        return pl.ds(pl.multiple_of(chunk * rows, rows), rows)

    def slot(at, chunk):
        return others.at[at_rows(chunk), pl.ds((at - 1) * width, width)]

    def to_across(chunk):
        return remote(mixed.at[at_rows(chunk), :], slot(2, chunk), send_sem.at[0, chunk], recv_sem.at[0, chunk], "head", across)

    def to_sibling(chunk):
        return remote(mixed.at[at_rows(chunk), :], slot(1, chunk), send_sem.at[1, chunk], recv_sem.at[1, chunk], "head", sibling)

    def relay(chunk):
        return remote(slot(2, chunk), slot(3, chunk), send_sem.at[2, chunk], recv_sem.at[2, chunk], "head", sibling)

    def carry_copy(flip, device):
        return pltpu.make_async_remote_copy(
            src_ref=mixed.at[pl.ds(count - CARRY_ROWS, CARRY_ROWS), :],
            dst_ref=carry.at[:, pl.ds(flip * width, width)],
            send_sem=carry_send.at[flip],
            recv_sem=carry_recv.at[flip],
            device_id={"seq": after, "head": device},
            device_id_type=MESH,
        )

    carries = [carry_copy(flip, device) for flip, device in enumerate((me, sibling, across, diagonal))]
    lane_head = lax.broadcasted_iota(jnp.int32, (rows, width), 1) // HEAD_DIM
    row = lax.broadcasted_iota(jnp.int32, (rows, rows), 0)
    column = lax.broadcasted_iota(jnp.int32, (rows, rows), 1)

    def attend(chunk):
        begin = pl.multiple_of(chunk * rows, rows)
        keys = k_ref[pl.ds(begin, span), :]
        values = v_ref[pl.ds(begin, span), :]
        query = q_ref[at_rows(chunk), :]
        floor = jnp.where(place == 0, WINDOW - begin, 0)
        result = jnp.zeros((rows, width), jnp.float32)
        for head in range(heads):
            masked_q = jnp.where(lane_head == head, query, jnp.zeros_like(query))
            scores = transposed_dot(masked_q, keys)
            pieces = []
            for at in range(0, span, rows):
                piece = scores[:, at : at + rows]
                if at == span - rows:
                    allowed = column <= row
                else:
                    allowed = column >= floor - at
                    if at == 0:
                        allowed = allowed & (column > row)
                pieces.append(jnp.where(allowed, piece, masked_low))
            top = pieces[0]
            for piece in pieces[1:]:
                top = jnp.maximum(top, piece)
            top = jnp.max(top, axis=1, keepdims=True)
            weights = [jnp.exp2((piece - top) * EXP2_SCALE) for piece in pieces]
            total = weights[0]
            for piece in weights[1:]:
                total = total + piece
            total = jnp.sum(total, axis=1, keepdims=True)
            rounded = jnp.concatenate([piece.astype(jnp.bfloat16) for piece in weights], axis=1)
            out = jnp.dot(rounded, values, preferred_element_type=jnp.float32)
            result = jnp.where(lane_head == head, out / total, result)
        mixed[at_rows(chunk), :] = result.astype(jnp.bfloat16)

    def one_chunk(chunk, state):
        attend(chunk)
        to_across(chunk).start()
        to_sibling(chunk).start()

        @pl.when(chunk > 0)
        def _():
            to_across(chunk - 1).wait_recv()
            relay(chunk - 1).start()

        return state

    lax.fori_loop(0, chunks, one_chunk, 0)

    @pl.when(has_next)
    def _():
        for copy in carries:
            copy.start()

    to_across(chunks - 1).wait_recv()
    relay(chunks - 1).start()

    def finish_chunk(chunk, state):
        to_sibling(chunk).wait_recv()
        relay(chunk).wait_recv()
        merged = jnp.dot(mixed[at_rows(chunk), :], cols_ref[:width, :], preferred_element_type=jnp.float32)
        merged = merged + jnp.dot(others[at_rows(chunk), :], cols_ref[width:, :], preferred_element_type=jnp.float32)
        begin = pl.multiple_of(CARRY_ROWS + chunk * rows, CARRY_ROWS)
        value = (start_ref[pl.ds(begin, rows), :].astype(jnp.float32) + merged).astype(jnp.bfloat16)
        fine_ref[at_rows(chunk), :] = value
        for lane in range(width // 128):
            stream[lane, pl.ds(begin, rows), :] = value[:, lane * 128 : lane * 128 + 128].astype(jnp.float32)
        return state

    lax.fori_loop(0, chunks, finish_chunk, 0)

    @pl.when(place == 0)
    def _():
        stream[:, 0:CARRY_ROWS, :] = jnp.zeros((width // 128, CARRY_ROWS, 128), jnp.float32)

    @pl.when(place > 0)
    def _():
        for copy in carries:
            copy.wait_recv()
        merged = jnp.dot(carry[...], cols_ref[...], preferred_element_type=jnp.float32)
        value = (start_ref[0:CARRY_ROWS, :].astype(jnp.float32) + merged).astype(jnp.bfloat16)
        for lane in range(width // 128):
            stream[lane, 0:CARRY_ROWS, :] = value[:, lane * 128 : lane * 128 + 128].astype(jnp.float32)

    groups = count // SHORTEN
    total = jnp.zeros((groups, w_ref.shape[2]), jnp.float32)
    for offset in range(SHORTEN):
        begin = CARRY_ROWS - (SHORTEN - 1) + offset
        member = jnp.concatenate(
            [stream[lane, pl.ds(begin, groups, stride=SHORTEN), :] for lane in range(width // 128)], axis=1
        )
        total = total + jnp.dot(member.astype(jnp.bfloat16), w_ref[offset], preferred_element_type=jnp.float32)
    part_ref[...] = total

    def drain(chunk, state):
        to_across(chunk).wait_send()
        to_sibling(chunk).wait_send()
        relay(chunk).wait_send()
        return state

    lax.fori_loop(0, chunks, drain, 0)

    @pl.when(has_next)
    def _():
        for copy in carries:
            copy.wait_send()


def fine_stage(query, keys, values, start, columns, weights):
    count, width = query.shape
    chunks = count // min(256, count)
    return pl.pallas_call(
        fine_kernel,
        out_shape=(
            jax.ShapeDtypeStruct((count // SHORTEN, weights.shape[2]), jnp.float32),
            jax.ShapeDtypeStruct((count, width), jnp.bfloat16),
        ),
        in_specs=[VMEM_SPEC] * 6,
        out_specs=(VMEM_SPEC, VMEM_SPEC),
        scratch_shapes=[
            pltpu.VMEM((count, width), jnp.bfloat16),
            pltpu.VMEM((count, 3 * width), jnp.bfloat16),
            pltpu.VMEM((CARRY_ROWS, 4 * width), jnp.bfloat16),
            pltpu.VMEM((width // 128, CARRY_ROWS + count, 128), jnp.float32),
            pltpu.SemaphoreType.DMA((3, chunks)),
            pltpu.SemaphoreType.DMA((3, chunks)),
            pltpu.SemaphoreType.DMA((4,)),
            pltpu.SemaphoreType.DMA((4,)),
        ],
        compiler_params=pltpu.CompilerParams(
            collective_id=1, has_side_effects=True, vmem_limit_bytes=48 * 2**20
        ),
        name="fine_stage",
    )(query, keys, values, start, columns, weights)


PIECES = 2


def head_sum(part_ref, residual_ref, out_ref, send_a, recv_a, send_b, recv_b, final, send_sem, recv_sem):
    me, sibling, across, diagonal = head_peers()
    rows, width = final.shape
    size = rows // PIECES

    def columns(place):
        return pl.ds(pl.multiple_of(place * width, width), width)

    def piece_rows(piece):
        return pl.ds(piece * size, size)

    def copy_of(kind, piece, source, target, device):
        return remote(source, target, send_sem.at[kind, piece], recv_sem.at[kind, piece], "head", device)

    first, second, to_across, to_sibling, relays = [], [], [], [], []
    for slot, owner in enumerate((diagonal, sibling)):
        for piece in range(PIECES):
            at = piece_rows(piece)
            send_a[slot, at, :] = part_ref[at, columns(owner)].astype(send_a.dtype)
            copy = copy_of(slot, piece, send_a.at[slot, at, :], recv_a.at[slot, at, :], sibling)
            copy.start()
            first.append(copy)
    for piece in range(PIECES):
        at = piece_rows(piece)
        first[piece].wait_recv()
        send_b[at, :] = (part_ref[at, columns(across)] + recv_a[0, at, :].astype(jnp.float32)).astype(send_b.dtype)
        copy = copy_of(2, piece, send_b.at[at, :], recv_b.at[at, :], across)
        copy.start()
        second.append(copy)
    for piece in range(PIECES):
        at = piece_rows(piece)
        first[PIECES + piece].wait_recv()
        total = part_ref[at, columns(me)] + recv_a[1, at, :].astype(jnp.float32)
        if residual_ref is not None:
            total = total + residual_ref[at, columns(me)].astype(jnp.float32)
        second[piece].wait_recv()
        total = total + recv_b[at, :].astype(jnp.float32)
        final[at, :] = total.astype(final.dtype)
        copy = copy_of(3, piece, final.at[at, :], out_ref.at[at, columns(me)], across)
        copy.start()
        to_across.append(copy)
        copy = copy_of(4, piece, final.at[at, :], out_ref.at[at, columns(me)], sibling)
        copy.start()
        to_sibling.append(copy)
        out_ref[at, columns(me)] = final[at, :]
    for piece in range(PIECES):
        to_across[piece].wait_recv()
        block = out_ref.at[piece_rows(piece), columns(across)]
        copy = copy_of(5, piece, block, block, sibling)
        copy.start()
        relays.append(copy)
    for copy in first + second + to_across:
        copy.wait_send()
    for copy in to_sibling + relays:
        copy.wait()


def coarse_body(
    short_ref, gain_ref, wq_ref, wk_ref, wv_ref, wo_ref, part_ref, loaded,
    pairs, queries, top_ref, total_ref, acc_ref, up_send, up_recv, cross_send, cross_recv,
):
    count, rows, both = pairs.shape
    width = both // 2
    heads = width // HEAD_DIM
    levels = count // 2
    place = lax.axis_index("seq")
    side = place % 2
    level = place // 2
    cross = place + 1 - 2 * side
    above = (place + 2) % count
    has_above = level < levels - 1

    lanes = min(128, width)
    lane = lax.broadcasted_iota(jnp.int32, (rows, lanes), 1) % HEAD_DIM
    half_lane = lane % (HEAD_DIM // 2)
    period_log = 4 + (half_lane * 14) // (HEAD_DIM // 2)
    period = jnp.left_shift(jnp.ones_like(period_log), period_log)
    position = place * rows + lax.broadcasted_iota(jnp.int32, (rows, lanes), 0)
    cycle = jnp.bitwise_and(position, period - 1).astype(jnp.float32)
    angle = cycle * (2.0 * math.pi / period.astype(jnp.float32))
    reps = width // lanes
    cosine = jnp.concatenate([jnp.cos(angle)] * reps, axis=1)
    signed = jnp.where(lane < HEAD_DIM // 2, -jnp.sin(angle), jnp.sin(angle))
    sine = jnp.concatenate([signed] * reps, axis=1)
    is_lower = lax.broadcasted_iota(jnp.int32, (rows, width), 1) % HEAD_DIM < HEAD_DIM // 2

    def turned(values):
        other = jnp.where(
            is_lower,
            pltpu.roll(values, width - HEAD_DIM // 2, 1),
            pltpu.roll(values, HEAD_DIM // 2, 1),
        )
        return (values * cosine + other * sine).astype(jnp.bfloat16)

    data = short_ref[...].astype(jnp.float32)
    power = jnp.mean(data * data, axis=1, keepdims=True)
    coarse_in = (data * lax.rsqrt(power + epsilon) * gain_ref[...]).astype(jnp.bfloat16)
    for copy in loaded:
        copy.wait()
    own = pairs.at[place]
    own[:, :width] = turned(jnp.dot(coarse_in, wk_ref[...], preferred_element_type=jnp.float32))
    own[:, width:] = jnp.dot(coarse_in, wv_ref[...], preferred_element_type=jnp.float32).astype(jnp.bfloat16)

    def up(source_level):
        block = pairs.at[2 * source_level + side]
        return remote(block, block, up_send.at[source_level], up_recv.at[source_level], "seq", above)

    def over(source_level, source_side):
        block = pairs.at[2 * source_level + source_side]
        return remote(block, block, cross_send.at[source_level], cross_recv.at[source_level], "seq", cross)

    @pl.when(has_above)
    def _():
        up(level).start()

    @pl.when(side == 0)
    def _():
        over(level, 0).start()

    query = turned(jnp.dot(coarse_in, wq_ref[...], preferred_element_type=jnp.float32))
    lane_head = lax.broadcasted_iota(jnp.int32, (rows, width), 1) // HEAD_DIM
    for head in range(heads):
        queries[head * rows : (head + 1) * rows, :] = jnp.where(
            lane_head == head, query, jnp.zeros_like(query)
        )

    def absorb(block, diagonal):
        keys = pairs[block, :, :width]
        values = pairs[block, :, width:]
        for head in range(heads):
            part = slice(head * rows, (head + 1) * rows)
            scores = transposed_dot(queries[part, :], keys)
            if diagonal:
                row = lax.broadcasted_iota(jnp.int32, scores.shape, 0)
                column = lax.broadcasted_iota(jnp.int32, scores.shape, 1)
                scores = jnp.where(column <= row, scores, masked_low)
            fresh = jnp.max(scores, axis=1, keepdims=True)
            if not diagonal:
                fresh = jnp.maximum(top_ref[part, :], fresh)
            weights = jnp.exp2((scores - fresh) * EXP2_SCALE)
            total = jnp.sum(weights, axis=1, keepdims=True)
            mixed = jnp.dot(weights.astype(jnp.bfloat16), values, preferred_element_type=jnp.float32)
            if not diagonal:
                factor = jnp.exp2((top_ref[part, :] - fresh) * EXP2_SCALE)
                total = total + total_ref[part, :] * factor
                mixed = mixed + acc_ref[part, :] * factor
            top_ref[part, :] = fresh
            total_ref[part, :] = total
            acc_ref[part, :] = mixed

    absorb(place, True)

    def take_over(source_level):
        over(source_level, 1 - side).wait_recv()
        absorb(2 * source_level + 1 - side, False)

    def one_level(step, state):
        source_level = level - 1 - step
        up(source_level).wait_recv()

        @pl.when(has_above)
        def _():
            up(source_level).start()

        over(source_level, side).start()
        absorb(2 * source_level + side, False)

        @pl.when((step > 0) | (side == 1))
        def _():
            take_over(source_level + 1)

        return state

    lax.fori_loop(0, level, one_level, 0)

    @pl.when((level > 0) | (side == 1))
    def _():
        take_over(0)

    result = jnp.zeros((rows, width), jnp.float32)
    for head in range(heads):
        part = slice(head * rows, (head + 1) * rows)
        result = jnp.where(lane_head == head, acc_ref[part, :] / total_ref[part, :], result)
    part_ref[...] = jnp.dot(result.astype(jnp.bfloat16), wo_ref[...], preferred_element_type=jnp.float32)

    def drain(step, state):
        source_level = level - 1 - step

        @pl.when(has_above)
        def _():
            up(source_level).wait_send()

        over(source_level, side).wait_send()
        return state

    lax.fori_loop(0, level, drain, 0)

    @pl.when(has_above)
    def _():
        up(level).wait_send()

    @pl.when(side == 0)
    def _():
        over(level, 0).wait_send()


def tail_kernel(
    short_part, coarse_gain, ffn_gain, fine_ref, wq, wk, wv, wo, w_up, w_down, w_lift, out_ref,
    wq_v, wk_v, wv_v, wo_v, up_v, down_v, lift_v, load_sem,
    part, short, summed, first, second, spread, send_a, recv_a, send_b, recv_b, final, sum_send, sum_recv,
    *coarse_scratch,
):
    count = lax.axis_size("seq")
    place = lax.axis_index("seq")
    me, sibling, across, diagonal = head_peers()
    loads = [
        pltpu.make_async_copy(source, target, load_sem.at[index])
        for index, (source, target) in enumerate(
            ((wq, wq_v), (wk, wk_v), (wv, wv_v), (wo, wo_v), (w_up, up_v), (w_down, down_v), (w_lift, lift_v))
        )
    ]
    for copy in loads:
        copy.start()
    barrier = pltpu.get_barrier_semaphore()
    for device in (sibling, across):
        pl.semaphore_signal(barrier, inc=1, device_id={"head": device}, device_id_type=MESH)
    for device in (place + 1 - 2 * (place % 2), (place + 2) % count, (place + count - 2) % count):
        pl.semaphore_signal(barrier, inc=1, device_id={"seq": device}, device_id_type=MESH)
    pl.semaphore_wait(barrier, 5)

    def summing(index, source, residual, target):
        head_sum(
            source, residual, target, send_a.at[index], recv_a.at[index], send_b.at[index],
            recv_b.at[index], final.at[index], sum_send.at[index], sum_recv.at[index],
        )

    summing(0, short_part, None, short)
    coarse_body(short, coarse_gain, wq_v, wk_v, wv_v, wo_v, part, loads[:4], *coarse_scratch)
    summing(1, part, None, summed)
    value = short[...].astype(jnp.float32) + summed[...].astype(jnp.float32)
    first[...] = value
    power = jnp.mean(value * value, axis=1, keepdims=True)
    normed = (value * lax.rsqrt(power + epsilon) * ffn_gain[...]).astype(jnp.bfloat16)
    for copy in loads[4:]:
        copy.wait()
    inner = jax.nn.gelu(jnp.dot(normed, up_v[...], preferred_element_type=jnp.float32)).astype(jnp.bfloat16)
    part[...] = jnp.dot(inner, down_v[...], preferred_element_type=jnp.float32)
    summing(2, part, first, second)

    groups = second.shape[0]
    width = fine_ref.shape[1]
    for member in range(SHORTEN):
        lifted = jnp.dot(
            second[...], lift_v[:, member * width : (member + 1) * width], preferred_element_type=jnp.float32
        )
        for lane in range(width // 128):
            spread[lane, pl.ds(member, groups, stride=SHORTEN), :] = lifted[:, lane * 128 : lane * 128 + 128]
    for lane in range(width // 128):
        piece = slice(lane * 128, lane * 128 + 128)
        out_ref[:, piece] = (fine_ref[:, piece].astype(jnp.float32) + spread[lane]).astype(jnp.bfloat16)


def tail_stage(short_part, coarse_gain, ffn_gain, fine, *weights):
    rows, full = short_part.shape
    width = fine.shape[1]
    heads = width // HEAD_DIM
    count = lax.axis_size("seq")
    block = (3, rows, full // 4)
    return pl.pallas_call(
        tail_kernel,
        out_shape=jax.ShapeDtypeStruct(fine.shape, fine.dtype),
        in_specs=[VMEM_SPEC] * 4 + [pl.BlockSpec(memory_space=pl.ANY)] * len(weights),
        out_specs=VMEM_SPEC,
        scratch_shapes=[pltpu.VMEM(weight.shape, weight.dtype) for weight in weights]
        + [
            pltpu.SemaphoreType.DMA((len(weights),)),
            pltpu.VMEM((rows, full), jnp.float32),
            pltpu.VMEM((rows, full), jnp.bfloat16),
            pltpu.VMEM((rows, full), jnp.bfloat16),
            pltpu.VMEM((rows, full), jnp.float32),
            pltpu.VMEM((rows, full), jnp.bfloat16),
            pltpu.VMEM((width // 128, fine.shape[0], 128), jnp.float32),
            pltpu.VMEM((3, 2) + block[1:], jnp.bfloat16),
            pltpu.VMEM((3, 2) + block[1:], jnp.bfloat16),
            pltpu.VMEM(block, jnp.bfloat16),
            pltpu.VMEM(block, jnp.bfloat16),
            pltpu.VMEM(block, jnp.bfloat16),
            pltpu.SemaphoreType.DMA((3, 6, PIECES)),
            pltpu.SemaphoreType.DMA((3, 6, PIECES)),
            pltpu.VMEM((count, rows, 2 * width), jnp.bfloat16),
            pltpu.VMEM((heads * rows, width), jnp.bfloat16),
            pltpu.VMEM((heads * rows, 1), jnp.float32),
            pltpu.VMEM((heads * rows, 1), jnp.float32),
            pltpu.VMEM((heads * rows, width), jnp.float32),
        ]
        + [pltpu.SemaphoreType.DMA((count // 2,)) for _ in range(4)],
        compiler_params=pltpu.CompilerParams(
            collective_id=2, has_side_effects=True, vmem_limit_bytes=44 * 2**20
        ),
        name="tail_stage",
    )(short_part, coarse_gain, ffn_gain, fine, *weights)


def local(
    token_ids,
    embedding,
    fine_norm,
    fine_query,
    fine_key,
    fine_value,
    fine_output,
    shorten_weight,
    coarse_norm,
    coarse_query,
    coarse_key,
    coarse_value,
    coarse_output,
    ffn_norm,
    ffn_up,
    ffn_down,
    upsample_weight,
):
    row_count = token_ids.shape[0]
    seq_place = lax.axis_index("seq")
    head_count = lax.axis_size("head")
    head_place = lax.axis_index("head")
    share = D // head_count
    column_start = head_place * share
    width = fine_query.shape[1]

    prior_ids = shifted(token_ids, "seq", 1)
    column_parts = [lax.dynamic_slice_in_dim(fine_output, column_start, share, 1)]
    for flip in range(1, head_count):
        piece = lax.dynamic_slice_in_dim(fine_output, (head_place ^ flip) * share, share, 1)
        column_parts.append(
            lax.ppermute(piece, "head", [(source, source ^ flip) for source in range(head_count)])
        )
    column_rows = jnp.concatenate(column_parts)

    level_in = rms_scale(embedding, fine_norm)
    level_q = project(level_in, fine_query)
    level_k = project(level_in, fine_key)
    level_v = project(level_in, fine_value).astype(jnp.bfloat16)
    own_levels = lax.dynamic_slice_in_dim(embedding, column_start, share, 1)
    k_table = jnp.concatenate([*split_two(level_k), *split_two(swapped(level_k)), level_v], axis=1)
    q_table = jnp.concatenate([*split_two(level_q), *split_two(swapped(level_q)), own_levels], axis=1)
    levels = jnp.arange(embedding.shape[0], dtype=jnp.int32)
    both_ids = jnp.concatenate([prior_ids, token_ids])
    one_hot = (both_ids[:, None] == levels[None, :]).astype(jnp.bfloat16)
    cosine, sine = turn_tables((seq_place - 1) * row_count, 2 * row_count, width)

    def rotated(joined, cos_rows, sin_rows):
        plain = joined[:, :width] + joined[:, width : 2 * width]
        other = joined[:, 2 * width : 3 * width] + joined[:, 3 * width : 4 * width]
        return (plain * cos_rows + other * sin_rows).astype(jnp.bfloat16)

    k_rows = project(one_hot, k_table)
    q_rows = project(one_hot[row_count - CARRY_ROWS :], q_table)
    fine_k = rotated(k_rows, cosine, sine)
    fine_v = k_rows[:, 4 * width :].astype(jnp.bfloat16)
    fine_q = rotated(q_rows[CARRY_ROWS:], cosine[row_count:], sine[row_count:])
    own_start = q_rows[:, 4 * width :].astype(jnp.bfloat16)
    short_part, fine = fine_stage(fine_q, fine_k, fine_v, own_start, column_rows, shorten_weight)
    return tail_stage(
        short_part,
        coarse_norm.reshape(1, D),
        ffn_norm.reshape(1, D),
        fine,
        coarse_query,
        coarse_key,
        coarse_value,
        coarse_output,
        ffn_up,
        ffn_down,
        upsample_weight.reshape(D, SHORTEN * share),
    )


def solution(mesh):
    return jax.shard_map(
        local,
        mesh=mesh,
        in_specs=(
            P("seq"),
            P(),
            P(),
            P(None, "head"),
            P(None, "head"),
            P(None, "head"),
            P("head", None),
            P(None, "head", None),
            P(),
            P(None, "head"),
            P(None, "head"),
            P(None, "head"),
            P("head", None),
            P(),
            P(None, "head"),
            P("head", None),
            P(None, None, "head"),
        ),
        out_specs=P("seq", "head"),
        check_vma=False,
    )
```

```python
import math

import jax
import jax.numpy as jnp
from jax import lax
from jax.experimental import pallas as pl
from jax.experimental.pallas import tpu as pltpu
from jax.sharding import PartitionSpec as P

D = 1024
HEAD_DIM = 64
SHORTEN = 4
WINDOW = 1024


epsilon = 1e-06
masked_low = -1e30
MESH = pl.DeviceIdType.MESH
EXP2_SCALE = HEAD_DIM ** (-0.5) * math.log2(math.e)
VMEM_SPEC = pl.BlockSpec(memory_space=pltpu.VMEM)


def shifted(value, axis, steps):
    count = lax.axis_size(axis)
    first, last = (max(0, -steps), min(count, count - steps))
    return lax.ppermute(value, axis, [(source, source + steps) for source in range(first, last)])


def project(left, right):
    return jnp.dot(left, right, preferred_element_type=jnp.float32)


def rms_scale(values, gain):
    data = values.astype(jnp.float32)
    power = jnp.mean(data * data, axis=-1, keepdims=True)
    return (data * lax.rsqrt(power + epsilon) * gain).astype(jnp.bfloat16)


def column_periods(width):
    halfway = HEAD_DIM // 2
    column_index = jnp.arange(width, dtype=jnp.int32) % halfway
    return 2 ** (4 + column_index * 14 // halfway)


def angles(positions, width):
    periods = column_periods(width)
    cycle = (positions[:, None] % periods[None, :]).astype(jnp.float32)
    return cycle * (2.0 * math.pi / periods.astype(jnp.float32))[None, :]


def turn_tables(begin, rows, width):
    lanes = min(128, width)
    fine_rows = min(64, rows)
    coarse = angles(begin + fine_rows * jnp.arange(rows // fine_rows, dtype=jnp.int32), lanes)
    small = angles(jnp.arange(fine_rows, dtype=jnp.int32), lanes)
    sign = jnp.where(jnp.arange(lanes) % HEAD_DIM < HEAD_DIM // 2, -1.0, 1.0).astype(jnp.float32)
    cos_a, sin_a = jnp.cos(coarse)[:, None, :], jnp.sin(coarse)[:, None, :]
    cos_b, sin_b = jnp.cos(small)[None], jnp.sin(small)[None]
    cosine = (cos_a * cos_b - sin_a * sin_b).reshape(rows, lanes)
    sine = ((sin_a * cos_b + cos_a * sin_b) * sign).reshape(rows, lanes)
    reps = width // lanes
    return jnp.tile(cosine, (1, reps)), jnp.tile(sine, (1, reps))


def swapped(values):
    halfway = HEAD_DIM // 2
    pieces = []
    for start in range(0, values.shape[1], HEAD_DIM):
        pieces.append(values[:, start + halfway : start + HEAD_DIM])
        pieces.append(values[:, start : start + halfway])
    return jnp.concatenate(pieces, axis=1)


def split_two(values):
    high = lax.reduce_precision(values, 8, 7)
    low = lax.reduce_precision(values - high, 8, 7)
    return high.astype(jnp.bfloat16), low.astype(jnp.bfloat16)


def transposed_dot(left, right):
    return lax.dot_general(
        left, right, (((1,), (1,)), ((), ())), preferred_element_type=jnp.float32
    )


def head_peers():
    me = lax.axis_index("head")
    sibling = me + 1 - 2 * (me % 2)
    across = (me + 2) % 4
    diagonal = (sibling + 2) % 4
    return me, sibling, across, diagonal


def remote(source, target, send, receive, axis, device):
    return pltpu.make_async_remote_copy(
        src_ref=source,
        dst_ref=target,
        send_sem=send,
        recv_sem=receive,
        device_id={axis: device},
        device_id_type=MESH,
    )


CARRY_ROWS = 16


def fine_kernel(
    q_ref, k_ref, v_ref, start_ref, rows_ref, w_ref, part_ref, fine_ref,
    mixed, others, carry, stream, cols_ref, send_sem, recv_sem, carry_send, carry_recv,
    cols_own, cols_send, cols_recv,
):
    count, width = q_ref.shape
    rows = min(256, count)
    chunks = count // rows
    heads = width // HEAD_DIM
    span = WINDOW + rows
    seq_count = lax.axis_size("seq")
    place = lax.axis_index("seq")
    me, sibling, across, diagonal = head_peers()
    after = (place + 1) % seq_count
    before = (place + seq_count - 1) % seq_count
    has_next = place < seq_count - 1

    barrier = pltpu.get_barrier_semaphore()
    for device in (sibling, across, diagonal):
        pl.semaphore_signal(barrier, inc=1, device_id={"head": device}, device_id_type=MESH)
    for line in (after, before):
        for device in range(4):
            pl.semaphore_signal(
                barrier, inc=1, device_id={"seq": line, "head": device}, device_id_type=MESH
            )
    pl.semaphore_wait(barrier, 11)

    def own_columns(device):
        return rows_ref.at[:, pl.ds(pl.multiple_of(device * width, width), width)]

    columns_in = [
        remote(
            own_columns(device), cols_ref.at[pl.ds(flip * width, width), :],
            cols_send.at[flip], cols_recv.at[flip], "head", device,
        )
        for flip, device in ((2, across), (3, diagonal), (1, sibling))
    ]
    for copy in columns_in:
        copy.start()
    keep = pltpu.make_async_copy(own_columns(me), cols_ref.at[pl.ds(0, width), :], cols_own)
    keep.start()

    def at_rows(chunk):
        return pl.ds(pl.multiple_of(chunk * rows, rows), rows)

    def slot(at, chunk):
        return others.at[at_rows(chunk), pl.ds((at - 1) * width, width)]

    def to_across(chunk):
        return remote(mixed.at[at_rows(chunk), :], slot(2, chunk), send_sem.at[0, chunk], recv_sem.at[0, chunk], "head", across)

    def to_sibling(chunk):
        return remote(mixed.at[at_rows(chunk), :], slot(1, chunk), send_sem.at[1, chunk], recv_sem.at[1, chunk], "head", sibling)

    def relay(chunk):
        return remote(slot(2, chunk), slot(3, chunk), send_sem.at[2, chunk], recv_sem.at[2, chunk], "head", sibling)

    def carry_copy(flip, device):
        return pltpu.make_async_remote_copy(
            src_ref=mixed.at[pl.ds(count - CARRY_ROWS, CARRY_ROWS), :],
            dst_ref=carry.at[:, pl.ds(flip * width, width)],
            send_sem=carry_send.at[flip],
            recv_sem=carry_recv.at[flip],
            device_id={"seq": after, "head": device},
            device_id_type=MESH,
        )

    carries = [carry_copy(flip, device) for flip, device in enumerate((me, sibling, across, diagonal))]
    lane_head = lax.broadcasted_iota(jnp.int32, (rows, width), 1) // HEAD_DIM
    row = lax.broadcasted_iota(jnp.int32, (rows, rows), 0)
    column = lax.broadcasted_iota(jnp.int32, (rows, rows), 1)

    def attend(chunk):
        begin = pl.multiple_of(chunk * rows, rows)
        keys = k_ref[pl.ds(begin, span), :]
        values = v_ref[pl.ds(begin, span), :]
        query = q_ref[at_rows(chunk), :]
        floor = jnp.where(place == 0, WINDOW - begin, 0)
        result = jnp.zeros((rows, width), jnp.float32)
        for head in range(heads):
            masked_q = jnp.where(lane_head == head, query, jnp.zeros_like(query))
            scores = transposed_dot(masked_q, keys)
            pieces = []
            for at in range(0, span, rows):
                piece = scores[:, at : at + rows]
                if at == span - rows:
                    allowed = column <= row
                else:
                    allowed = column >= floor - at
                    if at == 0:
                        allowed = allowed & (column > row)
                pieces.append(jnp.where(allowed, piece, masked_low))
            top = pieces[0]
            for piece in pieces[1:]:
                top = jnp.maximum(top, piece)
            top = jnp.max(top, axis=1, keepdims=True)
            weights = [jnp.exp2((piece - top) * EXP2_SCALE) for piece in pieces]
            total = weights[0]
            for piece in weights[1:]:
                total = total + piece
            total = jnp.sum(total, axis=1, keepdims=True)
            rounded = jnp.concatenate([piece.astype(jnp.bfloat16) for piece in weights], axis=1)
            out = jnp.dot(rounded, values, preferred_element_type=jnp.float32)
            result = jnp.where(lane_head == head, out / total, result)
        mixed[at_rows(chunk), :] = result.astype(jnp.bfloat16)

    def one_chunk(chunk, state):
        attend(chunk)
        to_across(chunk).start()
        to_sibling(chunk).start()

        @pl.when(chunk > 0)
        def _():
            to_across(chunk - 1).wait_recv()
            relay(chunk - 1).start()

        return state

    lax.fori_loop(0, chunks, one_chunk, 0)

    @pl.when(has_next)
    def _():
        for copy in carries:
            copy.start()

    to_across(chunks - 1).wait_recv()
    relay(chunks - 1).start()
    keep.wait()
    for copy in columns_in:
        copy.wait()

    def finish_chunk(chunk, state):
        to_sibling(chunk).wait_recv()
        relay(chunk).wait_recv()
        merged = jnp.dot(mixed[at_rows(chunk), :], cols_ref[:width, :], preferred_element_type=jnp.float32)
        merged = merged + jnp.dot(others[at_rows(chunk), :], cols_ref[width:, :], preferred_element_type=jnp.float32)
        begin = pl.multiple_of(CARRY_ROWS + chunk * rows, CARRY_ROWS)
        value = (start_ref[pl.ds(begin, rows), :].astype(jnp.float32) + merged).astype(jnp.bfloat16)
        fine_ref[at_rows(chunk), :] = value
        for lane in range(width // 128):
            stream[lane, pl.ds(begin, rows), :] = value[:, lane * 128 : lane * 128 + 128].astype(jnp.float32)
        return state

    lax.fori_loop(0, chunks, finish_chunk, 0)

    @pl.when(place == 0)
    def _():
        stream[:, 0:CARRY_ROWS, :] = jnp.zeros((width // 128, CARRY_ROWS, 128), jnp.float32)

    @pl.when(place > 0)
    def _():
        for copy in carries:
            copy.wait_recv()
        merged = jnp.dot(carry[...], cols_ref[...], preferred_element_type=jnp.float32)
        value = (start_ref[0:CARRY_ROWS, :].astype(jnp.float32) + merged).astype(jnp.bfloat16)
        for lane in range(width // 128):
            stream[lane, 0:CARRY_ROWS, :] = value[:, lane * 128 : lane * 128 + 128].astype(jnp.float32)

    groups = count // SHORTEN
    total = jnp.zeros((groups, w_ref.shape[2]), jnp.float32)
    for offset in range(SHORTEN):
        begin = CARRY_ROWS - (SHORTEN - 1) + offset
        member = jnp.concatenate(
            [stream[lane, pl.ds(begin, groups, stride=SHORTEN), :] for lane in range(width // 128)], axis=1
        )
        total = total + jnp.dot(member.astype(jnp.bfloat16), w_ref[offset], preferred_element_type=jnp.float32)
    part_ref[...] = total

    def drain(chunk, state):
        to_across(chunk).wait_send()
        to_sibling(chunk).wait_send()
        relay(chunk).wait_send()
        return state

    lax.fori_loop(0, chunks, drain, 0)

    @pl.when(has_next)
    def _():
        for copy in carries:
            copy.wait_send()


def fine_stage(query, keys, values, start, columns, weights):
    count, width = query.shape
    chunks = count // min(256, count)
    return pl.pallas_call(
        fine_kernel,
        out_shape=(
            jax.ShapeDtypeStruct((count // SHORTEN, weights.shape[2]), jnp.float32),
            jax.ShapeDtypeStruct((count, width), jnp.bfloat16),
        ),
        in_specs=[VMEM_SPEC] * 6,
        out_specs=(VMEM_SPEC, VMEM_SPEC),
        scratch_shapes=[
            pltpu.VMEM((count, width), jnp.bfloat16),
            pltpu.VMEM((count, 3 * width), jnp.bfloat16),
            pltpu.VMEM((CARRY_ROWS, 4 * width), jnp.bfloat16),
            pltpu.VMEM((width // 128, CARRY_ROWS + count, 128), jnp.float32),
            pltpu.VMEM((4 * width, width), jnp.bfloat16),
            pltpu.SemaphoreType.DMA((3, chunks)),
            pltpu.SemaphoreType.DMA((3, chunks)),
            pltpu.SemaphoreType.DMA((4,)),
            pltpu.SemaphoreType.DMA((4,)),
            pltpu.SemaphoreType.DMA,
            pltpu.SemaphoreType.DMA((4,)),
            pltpu.SemaphoreType.DMA((4,)),
        ],
        compiler_params=pltpu.CompilerParams(
            collective_id=1, has_side_effects=True, vmem_limit_bytes=48 * 2**20
        ),
        name="fine_stage",
    )(query, keys, values, start, columns, weights)


PIECES = 2


def head_sum(part_ref, residual_ref, out_ref, send_a, recv_a, send_b, recv_b, final, send_sem, recv_sem):
    me, sibling, across, diagonal = head_peers()
    rows, width = final.shape
    size = rows // PIECES

    def columns(place):
        return pl.ds(pl.multiple_of(place * width, width), width)

    def piece_rows(piece):
        return pl.ds(piece * size, size)

    def copy_of(kind, piece, source, target, device):
        return remote(source, target, send_sem.at[kind, piece], recv_sem.at[kind, piece], "head", device)

    first, second, to_across, to_sibling, relays = [], [], [], [], []
    for slot, owner in enumerate((diagonal, sibling)):
        for piece in range(PIECES):
            at = piece_rows(piece)
            send_a[slot, at, :] = part_ref[at, columns(owner)].astype(send_a.dtype)
            copy = copy_of(slot, piece, send_a.at[slot, at, :], recv_a.at[slot, at, :], sibling)
            copy.start()
            first.append(copy)
    for piece in range(PIECES):
        at = piece_rows(piece)
        first[piece].wait_recv()
        send_b[at, :] = (part_ref[at, columns(across)] + recv_a[0, at, :].astype(jnp.float32)).astype(send_b.dtype)
        copy = copy_of(2, piece, send_b.at[at, :], recv_b.at[at, :], across)
        copy.start()
        second.append(copy)
    for piece in range(PIECES):
        at = piece_rows(piece)
        first[PIECES + piece].wait_recv()
        total = part_ref[at, columns(me)] + recv_a[1, at, :].astype(jnp.float32)
        if residual_ref is not None:
            total = total + residual_ref[at, columns(me)].astype(jnp.float32)
        second[piece].wait_recv()
        total = total + recv_b[at, :].astype(jnp.float32)
        final[at, :] = total.astype(final.dtype)
        copy = copy_of(3, piece, final.at[at, :], out_ref.at[at, columns(me)], across)
        copy.start()
        to_across.append(copy)
        copy = copy_of(4, piece, final.at[at, :], out_ref.at[at, columns(me)], sibling)
        copy.start()
        to_sibling.append(copy)
        out_ref[at, columns(me)] = final[at, :]
    for piece in range(PIECES):
        to_across[piece].wait_recv()
        block = out_ref.at[piece_rows(piece), columns(across)]
        copy = copy_of(5, piece, block, block, sibling)
        copy.start()
        relays.append(copy)
    for copy in first + second + to_across:
        copy.wait_send()
    for copy in to_sibling + relays:
        copy.wait()


def coarse_body(
    short_ref, gain_ref, wq_ref, wk_ref, wv_ref, wo_ref, part_ref, loaded,
    pairs, queries, top_ref, total_ref, acc_ref, up_send, up_recv, cross_send, cross_recv,
):
    count, rows, both = pairs.shape
    width = both // 2
    heads = width // HEAD_DIM
    levels = count // 2
    place = lax.axis_index("seq")
    side = place % 2
    level = place // 2
    cross = place + 1 - 2 * side
    above = (place + 2) % count
    has_above = level < levels - 1

    lanes = min(128, width)
    lane = lax.broadcasted_iota(jnp.int32, (rows, lanes), 1) % HEAD_DIM
    half_lane = lane % (HEAD_DIM // 2)
    period_log = 4 + (half_lane * 14) // (HEAD_DIM // 2)
    period = jnp.left_shift(jnp.ones_like(period_log), period_log)
    position = place * rows + lax.broadcasted_iota(jnp.int32, (rows, lanes), 0)
    cycle = jnp.bitwise_and(position, period - 1).astype(jnp.float32)
    angle = cycle * (2.0 * math.pi / period.astype(jnp.float32))
    reps = width // lanes
    cosine = jnp.concatenate([jnp.cos(angle)] * reps, axis=1)
    signed = jnp.where(lane < HEAD_DIM // 2, -jnp.sin(angle), jnp.sin(angle))
    sine = jnp.concatenate([signed] * reps, axis=1)
    is_lower = lax.broadcasted_iota(jnp.int32, (rows, width), 1) % HEAD_DIM < HEAD_DIM // 2

    def turned(values):
        other = jnp.where(
            is_lower,
            pltpu.roll(values, width - HEAD_DIM // 2, 1),
            pltpu.roll(values, HEAD_DIM // 2, 1),
        )
        return (values * cosine + other * sine).astype(jnp.bfloat16)

    data = short_ref[...].astype(jnp.float32)
    power = jnp.mean(data * data, axis=1, keepdims=True)
    coarse_in = (data * lax.rsqrt(power + epsilon) * gain_ref[...]).astype(jnp.bfloat16)
    for copy in loaded:
        copy.wait()
    own = pairs.at[place]
    own[:, :width] = turned(jnp.dot(coarse_in, wk_ref[...], preferred_element_type=jnp.float32))
    own[:, width:] = jnp.dot(coarse_in, wv_ref[...], preferred_element_type=jnp.float32).astype(jnp.bfloat16)

    def up(source_level):
        block = pairs.at[2 * source_level + side]
        return remote(block, block, up_send.at[source_level], up_recv.at[source_level], "seq", above)

    def over(source_level, source_side):
        block = pairs.at[2 * source_level + source_side]
        return remote(block, block, cross_send.at[source_level], cross_recv.at[source_level], "seq", cross)

    @pl.when(has_above)
    def _():
        up(level).start()

    @pl.when(side == 0)
    def _():
        over(level, 0).start()

    query = turned(jnp.dot(coarse_in, wq_ref[...], preferred_element_type=jnp.float32))
    lane_head = lax.broadcasted_iota(jnp.int32, (rows, width), 1) // HEAD_DIM
    for head in range(heads):
        queries[head * rows : (head + 1) * rows, :] = jnp.where(
            lane_head == head, query, jnp.zeros_like(query)
        )

    def absorb(block, diagonal):
        keys = pairs[block, :, :width]
        values = pairs[block, :, width:]
        for head in range(heads):
            part = slice(head * rows, (head + 1) * rows)
            scores = transposed_dot(queries[part, :], keys)
            if diagonal:
                row = lax.broadcasted_iota(jnp.int32, scores.shape, 0)
                column = lax.broadcasted_iota(jnp.int32, scores.shape, 1)
                scores = jnp.where(column <= row, scores, masked_low)
            fresh = jnp.max(scores, axis=1, keepdims=True)
            if not diagonal:
                fresh = jnp.maximum(top_ref[part, :], fresh)
            weights = jnp.exp2((scores - fresh) * EXP2_SCALE)
            total = jnp.sum(weights, axis=1, keepdims=True)
            mixed = jnp.dot(weights.astype(jnp.bfloat16), values, preferred_element_type=jnp.float32)
            if not diagonal:
                factor = jnp.exp2((top_ref[part, :] - fresh) * EXP2_SCALE)
                total = total + total_ref[part, :] * factor
                mixed = mixed + acc_ref[part, :] * factor
            top_ref[part, :] = fresh
            total_ref[part, :] = total
            acc_ref[part, :] = mixed

    absorb(place, True)

    def take_over(source_level):
        over(source_level, 1 - side).wait_recv()
        absorb(2 * source_level + 1 - side, False)

    def one_level(step, state):
        source_level = level - 1 - step
        up(source_level).wait_recv()

        @pl.when(has_above)
        def _():
            up(source_level).start()

        over(source_level, side).start()
        absorb(2 * source_level + side, False)

        @pl.when((step > 0) | (side == 1))
        def _():
            take_over(source_level + 1)

        return state

    lax.fori_loop(0, level, one_level, 0)

    @pl.when((level > 0) | (side == 1))
    def _():
        take_over(0)

    result = jnp.zeros((rows, width), jnp.float32)
    for head in range(heads):
        part = slice(head * rows, (head + 1) * rows)
        result = jnp.where(lane_head == head, acc_ref[part, :] / total_ref[part, :], result)
    part_ref[...] = jnp.dot(result.astype(jnp.bfloat16), wo_ref[...], preferred_element_type=jnp.float32)

    def drain(step, state):
        source_level = level - 1 - step

        @pl.when(has_above)
        def _():
            up(source_level).wait_send()

        over(source_level, side).wait_send()
        return state

    lax.fori_loop(0, level, drain, 0)

    @pl.when(has_above)
    def _():
        up(level).wait_send()

    @pl.when(side == 0)
    def _():
        over(level, 0).wait_send()


def tail_kernel(
    short_part, coarse_gain, ffn_gain, fine_ref, wq, wk, wv, wo, w_up, w_down, w_lift, out_ref,
    wq_v, wk_v, wv_v, wo_v, up_v, down_v, lift_v, load_sem,
    part, short, summed, first, second, spread, send_a, recv_a, send_b, recv_b, final, sum_send, sum_recv,
    *coarse_scratch,
):
    count = lax.axis_size("seq")
    place = lax.axis_index("seq")
    me, sibling, across, diagonal = head_peers()
    loads = [
        pltpu.make_async_copy(source, target, load_sem.at[index])
        for index, (source, target) in enumerate(
            ((wq, wq_v), (wk, wk_v), (wv, wv_v), (wo, wo_v), (w_up, up_v), (w_down, down_v), (w_lift, lift_v))
        )
    ]
    for copy in loads:
        copy.start()
    barrier = pltpu.get_barrier_semaphore()
    for device in (sibling, across):
        pl.semaphore_signal(barrier, inc=1, device_id={"head": device}, device_id_type=MESH)
    for device in (place + 1 - 2 * (place % 2), (place + 2) % count, (place + count - 2) % count):
        pl.semaphore_signal(barrier, inc=1, device_id={"seq": device}, device_id_type=MESH)
    pl.semaphore_wait(barrier, 5)

    def summing(index, source, residual, target):
        head_sum(
            source, residual, target, send_a.at[index], recv_a.at[index], send_b.at[index],
            recv_b.at[index], final.at[index], sum_send.at[index], sum_recv.at[index],
        )

    summing(0, short_part, None, short)
    coarse_body(short, coarse_gain, wq_v, wk_v, wv_v, wo_v, part, loads[:4], *coarse_scratch)
    summing(1, part, None, summed)
    value = short[...].astype(jnp.float32) + summed[...].astype(jnp.float32)
    first[...] = value
    power = jnp.mean(value * value, axis=1, keepdims=True)
    normed = (value * lax.rsqrt(power + epsilon) * ffn_gain[...]).astype(jnp.bfloat16)
    for copy in loads[4:]:
        copy.wait()
    inner = jax.nn.gelu(jnp.dot(normed, up_v[...], preferred_element_type=jnp.float32)).astype(jnp.bfloat16)
    part[...] = jnp.dot(inner, down_v[...], preferred_element_type=jnp.float32)
    summing(2, part, first, second)

    groups = second.shape[0]
    width = fine_ref.shape[1]
    for member in range(SHORTEN):
        lifted = jnp.dot(
            second[...], lift_v[:, member * width : (member + 1) * width], preferred_element_type=jnp.float32
        )
        for lane in range(width // 128):
            spread[lane, pl.ds(member, groups, stride=SHORTEN), :] = lifted[:, lane * 128 : lane * 128 + 128]
    for lane in range(width // 128):
        piece = slice(lane * 128, lane * 128 + 128)
        out_ref[:, piece] = (fine_ref[:, piece].astype(jnp.float32) + spread[lane]).astype(jnp.bfloat16)


def tail_stage(short_part, coarse_gain, ffn_gain, fine, *weights):
    rows, full = short_part.shape
    width = fine.shape[1]
    heads = width // HEAD_DIM
    count = lax.axis_size("seq")
    block = (3, rows, full // 4)
    return pl.pallas_call(
        tail_kernel,
        out_shape=jax.ShapeDtypeStruct(fine.shape, fine.dtype),
        in_specs=[VMEM_SPEC] * 4 + [pl.BlockSpec(memory_space=pl.ANY)] * len(weights),
        out_specs=VMEM_SPEC,
        scratch_shapes=[pltpu.VMEM(weight.shape, weight.dtype) for weight in weights]
        + [
            pltpu.SemaphoreType.DMA((len(weights),)),
            pltpu.VMEM((rows, full), jnp.float32),
            pltpu.VMEM((rows, full), jnp.bfloat16),
            pltpu.VMEM((rows, full), jnp.bfloat16),
            pltpu.VMEM((rows, full), jnp.float32),
            pltpu.VMEM((rows, full), jnp.bfloat16),
            pltpu.VMEM((width // 128, fine.shape[0], 128), jnp.float32),
            pltpu.VMEM((3, 2) + block[1:], jnp.bfloat16),
            pltpu.VMEM((3, 2) + block[1:], jnp.bfloat16),
            pltpu.VMEM(block, jnp.bfloat16),
            pltpu.VMEM(block, jnp.bfloat16),
            pltpu.VMEM(block, jnp.bfloat16),
            pltpu.SemaphoreType.DMA((3, 6, PIECES)),
            pltpu.SemaphoreType.DMA((3, 6, PIECES)),
            pltpu.VMEM((count, rows, 2 * width), jnp.bfloat16),
            pltpu.VMEM((heads * rows, width), jnp.bfloat16),
            pltpu.VMEM((heads * rows, 1), jnp.float32),
            pltpu.VMEM((heads * rows, 1), jnp.float32),
            pltpu.VMEM((heads * rows, width), jnp.float32),
        ]
        + [pltpu.SemaphoreType.DMA((count // 2,)) for _ in range(4)],
        compiler_params=pltpu.CompilerParams(
            collective_id=2, has_side_effects=True, vmem_limit_bytes=44 * 2**20
        ),
        name="tail_stage",
    )(short_part, coarse_gain, ffn_gain, fine, *weights)


def local(
    token_ids,
    embedding,
    fine_norm,
    fine_query,
    fine_key,
    fine_value,
    fine_output,
    shorten_weight,
    coarse_norm,
    coarse_query,
    coarse_key,
    coarse_value,
    coarse_output,
    ffn_norm,
    ffn_up,
    ffn_down,
    upsample_weight,
):
    row_count = token_ids.shape[0]
    seq_place = lax.axis_index("seq")
    head_count = lax.axis_size("head")
    head_place = lax.axis_index("head")
    share = D // head_count
    column_start = head_place * share
    width = fine_query.shape[1]

    prior_ids = shifted(token_ids, "seq", 1)
    level_in = rms_scale(embedding, fine_norm)
    level_q = project(level_in, fine_query)
    level_k = project(level_in, fine_key)
    level_v = project(level_in, fine_value).astype(jnp.bfloat16)
    own_levels = lax.dynamic_slice_in_dim(embedding, column_start, share, 1)
    k_table = jnp.concatenate([*split_two(level_k), *split_two(swapped(level_k)), level_v], axis=1)
    q_table = jnp.concatenate([*split_two(level_q), *split_two(swapped(level_q)), own_levels], axis=1)
    levels = jnp.arange(embedding.shape[0], dtype=jnp.int32)
    both_ids = jnp.concatenate([prior_ids, token_ids])
    one_hot = (both_ids[:, None] == levels[None, :]).astype(jnp.bfloat16)
    cosine, sine = turn_tables((seq_place - 1) * row_count, 2 * row_count, width)

    def rotated(joined, cos_rows, sin_rows):
        plain = joined[:, :width] + joined[:, width : 2 * width]
        other = joined[:, 2 * width : 3 * width] + joined[:, 3 * width : 4 * width]
        return (plain * cos_rows + other * sin_rows).astype(jnp.bfloat16)

    k_rows = project(one_hot, k_table)
    q_rows = project(one_hot[row_count - CARRY_ROWS :], q_table)
    fine_k = rotated(k_rows, cosine, sine)
    fine_v = k_rows[:, 4 * width :].astype(jnp.bfloat16)
    fine_q = rotated(q_rows[CARRY_ROWS:], cosine[row_count:], sine[row_count:])
    own_start = q_rows[:, 4 * width :].astype(jnp.bfloat16)
    short_part, fine = fine_stage(fine_q, fine_k, fine_v, own_start, fine_output, shorten_weight)
    return tail_stage(
        short_part,
        coarse_norm.reshape(1, D),
        ffn_norm.reshape(1, D),
        fine,
        coarse_query,
        coarse_key,
        coarse_value,
        coarse_output,
        ffn_up,
        ffn_down,
        upsample_weight.reshape(D, SHORTEN * share),
    )


def solution(mesh):
    return jax.shard_map(
        local,
        mesh=mesh,
        in_specs=(
            P("seq"),
            P(),
            P(),
            P(None, "head"),
            P(None, "head"),
            P(None, "head"),
            P("head", None),
            P(None, "head", None),
            P(),
            P(None, "head"),
            P(None, "head"),
            P(None, "head"),
            P("head", None),
            P(),
            P(None, "head"),
            P("head", None),
            P(None, None, "head"),
        ),
        out_specs=P("seq", "head"),
        check_vma=False,
    )
```
